128 devices in a mesh: rep: 8 (over y_hi, z), fsdp: 16 (over x, y_lo, core).
Axes of the slice: x: 4, y: 4 (y_hi: 2, y_lo: 2; y = y_hi * 2 + y_lo), z: 4, core: 2. Of those that a mesh axis runs over, the one named last changes fastest.
Arguments:
- delta_query: bfloat16 [8, 8192, 4096], P('rep', 'fsdp'), may hold values from -60 to 60
- delta_output: bfloat16 [8, 4096, 8192], P('rep', 'fsdp'), may hold values from -60 to 60
- master_query: float32 [8192, 4096], P('fsdp', 'rep'), may hold values from -6 to 6
- master_output: float32 [4096, 8192], P('fsdp', 'rep'), may hold values from -6 to 6
- moment_query: float32 [8192, 4096], P('fsdp', 'rep'), may hold values from -6 to 6
- moment_output: float32 [4096, 8192], P('fsdp', 'rep'), may hold values from -6 to 6
Outputs:
- weights_query: bfloat16 [8192, 4096], P('fsdp')
- weights_output: bfloat16 [4096, 8192], P('fsdp')
- master_next_query: float32 [8192, 4096], P('fsdp', 'rep')
- master_next_output: float32 [4096, 8192], P('fsdp', 'rep')
- moment_next_query: float32 [8192, 4096], P('fsdp', 'rep')
- moment_next_output: float32 [4096, 8192], P('fsdp', 'rep')
The draws below stay inside these ranges and needn't reach their ends.
All inputs are finite; a program needn't handle non-finite values.
Results may differ from the reference program's by a relative error of at most 0.006.
Values may be sent and summed in bfloat16 or wider, within the bound.
A program may use at most 128 MiB of HBM per device.

```python
import math
import jax
import jax.numpy as jnp

D = 8192
QW = 4096
REPS = 8


def scaled_changes(key, replicas, rows, columns):
    first, second = jax.random.split(key, 2)
    row_scale = 10.0 ** (jnp.arange(rows, dtype=jnp.float32) / max(rows - 1, 1))
    column_scale = jnp.exp(jax.random.uniform(second, (columns,), jnp.float32, 0.0, 2.302585))
    replica_scale = 3.0 ** (jnp.arange(replicas, dtype=jnp.float32) / max(replicas - 1, 1))
    noise = jnp.clip(jax.random.normal(first, (replicas, rows, columns), jnp.float32), -4.0, 4.0)
    overall = 0.05
    values = noise * overall * replica_scale[:, None, None] * row_scale[None, :, None] * column_scale[None, None, :]
    return values.astype(jnp.bfloat16)


def draw_delta_query(key, part):
    return scaled_changes(jax.random.fold_in(key, 11), REPS, D, QW)


def draw_delta_output(key, part):
    return scaled_changes(jax.random.fold_in(key, 23), REPS, QW, D)


def block_levels(stream_key, extent, pieces, smallest, largest):
    gain, own = 1.0, jax.random.fold_in(stream_key, 6)
    for axis_at, shards_of in pieces:
        draws = jnp.exp(jax.random.uniform(jax.random.fold_in(own, axis_at), (shards_of,), jnp.float32, smallest / len(pieces), largest / len(pieces)))
        gain = gain * jnp.repeat(draws, extent[axis_at] // shards_of).reshape([-1 if axis == axis_at else 1 for axis in range(len(extent))])
    return gain


def bell_draw(own_key, extent, width, most, cuts=(), held_as=jnp.bfloat16):
    level = block_levels(own_key, extent, cuts, -0.22, 0.18) if cuts else 1.0
    entries = jax.random.normal(own_key, extent, jnp.float32) * width * level
    return jnp.minimum(jnp.maximum(entries, -most), most).astype(held_as)


def setup_inputs(seed: int = 0) -> dict:
    key_list = jax.random.split(jax.random.key(seed), 7)
    return {
        "delta_query": draw_delta_query(jax.random.fold_in(key_list[6], 71), 0),
        "delta_output": draw_delta_output(jax.random.fold_in(key_list[6], 71), 0),
        "master_query": bell_draw(key_list[2], (D, QW), 1.0, 6.0, ((0, 16), (1, 8)), jnp.float32),
        "master_output": bell_draw(key_list[3], (QW, D), 1.0, 6.0, ((0, 16), (1, 8)), jnp.float32),
        "moment_query": bell_draw(key_list[4], (D, QW), 1.0, 6.0, ((0, 16), (1, 8)), jnp.float32),
        "moment_output": bell_draw(key_list[5], (QW, D), 1.0, 6.0, ((0, 16), (1, 8)), jnp.float32),
    }


def outer_update(mean, factor, master, moment):
    grad = factor * mean
    moment_next = 0.9 * moment + grad
    master_next = master - 0.7 * (grad + 0.9 * moment_next)
    return (master_next, moment_next)

def reference(delta_query, delta_output, master_query, master_output, moment_query, moment_output):
    summed_query = jnp.zeros((D, QW), jnp.float32)
    summed_output = jnp.zeros((QW, D), jnp.float32)
    for replica in range(REPS):
        summed_query = summed_query + delta_query[replica].astype(jnp.float32)
        summed_output = summed_output + delta_output[replica].astype(jnp.float32)
    mean_query = summed_query / REPS
    mean_output = summed_output / REPS
    square_sum = jnp.sum(mean_query * mean_query) + jnp.sum(mean_output * mean_output)
    limit = 0.25 * math.sqrt(2.0 * D * QW)
    factor = jnp.minimum(1.0, limit / jnp.sqrt(square_sum + 1e-06))
    master_next_query, moment_next_query = outer_update(mean_query, factor, master_query, moment_query)
    master_next_output, moment_next_output = outer_update(mean_output, factor, master_output, moment_output)
    return (master_next_query.astype(jnp.bfloat16), master_next_output.astype(jnp.bfloat16), master_next_query, master_next_output, moment_next_query, moment_next_output)
```

```python
import functools
import math

import jax
import jax.numpy as jnp
from jax import lax
from jax.experimental import pallas as pl
from jax.experimental.pallas import tpu as pltpu
from jax.sharding import PartitionSpec as P

MESH = pl.DeviceIdType.MESH
BF16, F32 = jnp.bfloat16, jnp.float32
LIMIT = 0.25 * math.sqrt(2.0 * 8192 * 4096)
FIRST_Z = 9 / 16
STEP = 16


class Part:
    def __init__(self, rows, columns, sign):
        self.rows, self.columns, self.sign = rows, columns, sign
        self.a = int(rows * FIRST_Z) // STEP * STEP
        self.b = rows - self.a

    def window(self, owner):
        return pl.ds(pl.multiple_of(owner * self.columns, self.columns), self.columns)


def over_rows(rows, body, carry=None):
    def step(i, carry):
        return body(pl.ds(pl.multiple_of(i * STEP, STEP), STEP), carry)

    return lax.fori_loop(0, rows // STEP, step, carry, unroll=2 if rows // STEP % 2 == 0 else 1)


def add_up(out, *terms):
    def body(rows, _):
        total = terms[0][rows, :].astype(F32)
        for term in terms[1:]:
            total = total + term[rows, :].astype(F32)
        out[rows, :] = total.astype(out.dtype)

    over_rows(out.shape[0], body)


def add_up_squares(out, *terms):
    def body(rows, squares):
        total = terms[0][rows, :].astype(F32)
        for term in terms[1:]:
            total = total + term[rows, :].astype(F32)
        out[rows, :] = total
        return squares + total * total

    columns = out.shape[1]
    squares = over_rows(out.shape[0], body, jnp.zeros((STEP, columns), F32))
    line = jnp.sum(squares, axis=0, keepdims=True)
    return functools.reduce(jnp.add, [line[:, k : k + 128] for k in range(0, columns, 128)])


def kernel(parts, *refs):
    delta, master, moment = refs[0:2], refs[2:4], refs[4:6]
    weights, master_next, moment_next = refs[6:8], refs[8:10], refs[10:12]
    at = 12
    bufs = []
    for p in parts:
        names = list(shapes(p))
        bufs.append(dict(zip(names, refs[at : at + len(names)])))
        at += len(names)
    line1, line2, send_sem, recv_sem, local_sem = refs[at:]

    rep, shard = lax.axis_index("rep"), lax.axis_index("fsdp")
    y_hi, z = rep // 4, lax.rem(rep, 4)
    x, y_lo, core = shard // 4, lax.rem(shard // 2, 2), lax.rem(shard, 2)

    def owner(across, dz):
        return (1 - y_hi if across else y_hi) * 4 + lax.rem(z + dz % 4, 4)

    def chip(dx=0, dy=0, dz=0, dc=0):
        y = lax.rem(y_hi * 2 + y_lo + dy, 4)
        there = lax.rem(x + dx, 4) * 4 + lax.rem(y, 2) * 2 + lax.rem(core + dc, 2)
        return (y // 2) * 4 + lax.rem(z + dz, 4), there

    flying, local = {}, []

    def send(key, src, dst, target):
        k = len(flying)
        flying[key] = pltpu.make_async_remote_copy(
            src, dst, send_sem.at[k], recv_sem.at[k], device_id=target, device_id_type=MESH
        )
        flying[key].start()

    def arrived(*key):
        flying[key].wait_recv()

    def along_z(key, src, dst, dz):
        send(key, src, dst, (owner(0, dz), shard))

    def along_y(key, src, dst):
        send(key, src, dst, (owner(1, 0), shard))

    def start_local(src, dst):
        copy = pltpu.make_async_copy(src, dst, local_sem.at[len(local)])
        copy.start()
        local.append(copy)
        return copy

    both = range(len(parts))
    rows_a = [pl.ds(0, p.a) for p in parts]
    rows_b = [pl.ds(p.a, p.b) for p in parts]
    s = [p.sign for p in parts]

    own_a, own_b, params = {}, {}, []
    for side in (0, 1):
        for j in (0, 1):
            for t in both:
                cut = delta[t].at[rows_a[t], parts[t].window(owner(1 - side, (1 - j) * s[t]))]
                own_a[t, j, side] = start_local(cut, bufs[t]["own_a"].at[j, side])
    for k in range(4):
        for t in both:
            cut = delta[t].at[rows_b[t], parts[t].window(owner(0, k * s[t]))]
            own_b[t, k] = start_local(cut, bufs[t]["own_b"].at[k])
    for t in both:
        params.append(start_local(master[t], bufs[t]["master"]))
        params.append(start_local(moment[t], bufs[t]["moment"]))

    plane = [(dy, dz) for dy in range(4) for dz in range(4)][1:]
    across = [(dx, dc) for dx in range(4) for dc in range(2)][1:]
    barrier = pltpu.get_barrier_semaphore()
    for dy, dz in plane:
        pl.semaphore_signal(barrier, inc=1, device_id=chip(dy=dy, dz=dz), device_id_type=MESH)
    for dx, dc in across:
        pl.semaphore_signal(barrier, inc=1, device_id=chip(dx=dx, dc=dc), device_id_type=MESH)
    pl.semaphore_wait(barrier, len(plane) + len(across))

    def raw_a(side, t):
        p, b = parts[t], bufs[t]
        src = delta[t].at[rows_a[t], p.window(owner(1 - side, 2))]
        along_z(("a2", side, t), src, b["a2"].at[side], s[t])

    def raw_a_alone(side, t):
        p, b = parts[t], bufs[t]
        src = delta[t].at[rows_a[t], p.window(owner(1 - side, -s[t]))]
        along_z(("a1", side, t), src, b["a1"].at[side], -s[t])

    def merge_a(side, t):
        b = bufs[t]
        arrived("a2", side, t)
        own_a[t, 0, side].wait()
        add_up(b["merged_a"].at[side], b["own_a"].at[0, side], b["a2"].at[side])
        along_z(("am", side, t), b["merged_a"].at[side], b["am"].at[side], s[t])

    def raw_b(k, t):
        p, b = parts[t], bufs[t]
        src = delta[t].at[rows_b[t], p.window(owner(1, k * s[t]))]
        along_y(("by", k, t), src, b["by"].at[k])

    for t in both:
        raw_a(0, t)
    for t in both:
        raw_b(2, t)
    for t in both:
        raw_a_alone(0, t)
    for k in (3, 1):
        for t in both:
            raw_b(k, t)
    for t in both:
        merge_a(0, t)
    for t in both:
        raw_a(1, t)
    for t in both:
        raw_a_alone(1, t)
    for t in both:
        b = bufs[t]
        arrived("by", 2, t)
        own_b[t, 2].wait()
        add_up(b["sum_b"].at[0], b["own_b"].at[2], b["by"].at[2])
        along_z(("b2", t), b["sum_b"].at[0], b["b2"], s[t])
    for t in both:
        b = bufs[t]
        arrived("by", 3, t)
        own_b[t, 3].wait()
        add_up(b["sum_b"].at[1], b["own_b"].at[3], b["by"].at[3])
        along_z(("b1", t), b["sum_b"].at[1], b["b1"], -s[t])
    for t in both:
        b = bufs[t]
        arrived("a1", 0, t)
        arrived("am", 0, t)
        own_a[t, 1, 0].wait()
        add_up(b["sum_a"], b["own_a"].at[1, 0], b["a1"].at[0], b["am"].at[0])
        along_y(("ay", t), b["sum_a"], b["ay"])
    for t in both:
        raw_b(0, t)
    for t in both:
        merge_a(1, t)
    for t in both:
        b = bufs[t]
        arrived("by", 1, t)
        arrived("b2", t)
        own_b[t, 1].wait()
        add_up(b["sum_b"].at[2], b["own_b"].at[1], b["by"].at[1], b["b2"])
        along_z(("bm", t), b["sum_b"].at[2], b["bm"], s[t])

    for copy in params:
        copy.wait()
    for t in both:
        b = bufs[t]

        def base(rows, _, b=b):
            b["master"][rows, :] = b["master"][rows, :] - 0.567 * b["moment"][rows, :]

        over_rows(parts[t].rows, base)

    line = jnp.zeros((1, 128), F32)
    for t in both:
        b, p = bufs[t], parts[t]
        arrived("a1", 1, t)
        arrived("am", 1, t)
        arrived("ay", t)
        own_a[t, 1, 1].wait()
        terms = (b["own_a"].at[1, 1], b["a1"].at[1], b["am"].at[1], b["ay"])
        line += add_up_squares(b["total"].at[rows_a[t]], *terms)
    for t in both:
        b, p = bufs[t], parts[t]
        arrived("by", 0, t)
        arrived("b1", t)
        arrived("bm", t)
        own_b[t, 0].wait()
        terms = (b["own_b"].at[0], b["by"].at[0], b["b1"], b["bm"])
        line += add_up_squares(b["total"].at[rows_b[t]], *terms)

    line1[pl.ds(0, 1)] = line
    for i, (dy, dz) in enumerate(plane):
        send(("n1", i), line1.at[pl.ds(0, 1)], line1.at[pl.ds(i + 1, 1)], chip(dy=dy, dz=dz))
    for i in range(len(plane)):
        arrived("n1", i)
    line2[pl.ds(0, 1)] = jnp.sum(line1[...], axis=0, keepdims=True)
    for i, (dx, dc) in enumerate(across):
        send(("n2", i), line2.at[pl.ds(0, 1)], line2.at[pl.ds(i + 1, 1)], chip(dx=dx, dc=dc))
    for i in range(len(across)):
        arrived("n2", i)
    square_sum = jnp.sum(line2[...], axis=(0, 1), keepdims=True) * (1.0 / 64.0)
    factor = jnp.minimum(1.0, LIMIT / jnp.sqrt(square_sum + 1e-06)) * 0.125

    def update(t, first, rows_here):
        b = bufs[t]
        scale = 1.33 * factor

        def body(rows, _):
            rows = pl.ds(pl.multiple_of(first + rows.start, STEP), STEP)
            new = b["master"][rows, :] - scale * b["total"][rows, :]
            b["master"][rows, :] = new
            b["weights"][rows, :] = new.astype(BF16)

        over_rows(rows_here, body)

    def out_at(t, rows, who):
        return weights[t].at[rows, parts[t].window(who)]

    def give(t, rows, dz, who, src=None):
        key = ("w", t, rows is rows_a[t], dz, who)
        dst = out_at(t, rows, owner(*who))
        src = dst if src is None else src
        if dz is None:
            along_y(key, src, dst)
        else:
            along_z(key, src, dst, dz)

    def got(t, rows, dz, who):
        arrived("w", t, rows is rows_a[t], dz, who)

    own = (0, 0)
    for t in both:
        update(t, 0, parts[t].a)
        give(t, rows_a[t], None, own, bufs[t]["weights"].at[rows_a[t]])
    for t in both:
        update(t, parts[t].a, parts[t].b)
        for dz in (s[t], -s[t]):
            give(t, rows_b[t], dz, own, bufs[t]["weights"].at[rows_b[t]])
    for t in both:
        give(t, rows_b[t], None, own, bufs[t]["weights"].at[rows_b[t]])
    for t in both:
        for dz in (s[t], -s[t]):
            give(t, rows_a[t], dz, own, bufs[t]["weights"].at[rows_a[t]])
    for t in both:
        start_local(bufs[t]["weights"], weights[t].at[:, parts[t].window(rep)])
        start_local(bufs[t]["master"], master_next[t])

    def next_moment(t):
        b = bufs[t]

        def body(rows, _):
            b["moment"][rows, :] = 0.9 * b["moment"][rows, :] + factor * b["total"][rows, :]

        over_rows(parts[t].rows, body)
        start_local(b["moment"], moment_next[t])

    for t in both:
        got(t, rows_b[t], s[t], own)
        give(t, rows_b[t], s[t], (0, -s[t]))
        give(t, rows_b[t], None, (0, -s[t]))
    for t in both:
        got(t, rows_b[t], -s[t], own)
        give(t, rows_b[t], None, (0, s[t]))
    for t in both:
        next_moment(t)
    for t in both:
        got(t, rows_a[t], None, own)
        for dz in (s[t], -s[t]):
            give(t, rows_a[t], dz, (1, 0))
    for t in both:
        got(t, rows_b[t], s[t], (0, -s[t]))
        give(t, rows_b[t], None, (0, 2))
    for t in both:
        got(t, rows_a[t], s[t], own)
        give(t, rows_a[t], s[t], (0, -s[t]))
    for t in both:
        got(t, rows_a[t], s[t], (1, 0))
        give(t, rows_a[t], s[t], (1, -s[t]))
    for t in both:
        got(t, rows_a[t], -s[t], own)
        got(t, rows_a[t], -s[t], (1, 0))
        got(t, rows_a[t], s[t], (0, -s[t]))
        got(t, rows_a[t], s[t], (1, -s[t]))
        for who in (own, (0, -s[t]), (0, s[t]), (0, 2)):
            got(t, rows_b[t], None, who)
    for copy in flying.values():
        copy.wait_send()
    for copy in local[-6:]:
        copy.wait()


def shapes(p):
    a, b, c = p.a, p.b, p.columns
    return {
        "own_a": (2, 2, a, c),
        "own_b": (4, b, c),
        "a2": (2, a, c),
        "a1": (2, a, c),
        "am": (2, a, c),
        "ay": (a, c),
        "merged_a": (2, a, c),
        "sum_a": (a, c),
        "by": (4, b, c),
        "b2": (b, c),
        "b1": (b, c),
        "bm": (b, c),
        "sum_b": (3, b, c),
        "total": (p.rows, c),
        "master": (p.rows, c),
        "moment": (p.rows, c),
        "weights": (p.rows, c),
    }


def scratch(p):
    wide = ("total", "master", "moment")
    return [pltpu.VMEM(shape, F32 if n in wide else BF16) for n, shape in shapes(p).items()]


def on_device(delta_query, delta_output, *params):
    deltas = (delta_query[0], delta_output[0])
    parts = (Part(*params[0].shape, 1), Part(*params[1].shape, -1))
    outs = [jax.ShapeDtypeStruct(d.shape, BF16) for d in deltas]
    outs += [jax.ShapeDtypeStruct(p.shape, F32) for p in params]
    anywhere = pl.BlockSpec(memory_space=pl.ANY)
    return pl.pallas_call(
        functools.partial(kernel, parts),
        out_shape=outs,
        in_specs=[anywhere] * 6,
        out_specs=[anywhere] * 6,
        scratch_shapes=[
            *scratch(parts[0]),
            *scratch(parts[1]),
            pltpu.VMEM((16, 128), F32),
            pltpu.VMEM((8, 128), F32),
            pltpu.SemaphoreType.DMA((80,)),
            pltpu.SemaphoreType.DMA((80,)),
            pltpu.SemaphoreType.DMA((32,)),
        ],
        compiler_params=pltpu.CompilerParams(collective_id=0, has_side_effects=True),
        name="outer_step",
    )(*deltas, *params)


def solution(mesh):
    placed = P("fsdp", "rep")
    return jax.shard_map(
        on_device,
        mesh=mesh,
        in_specs=(P("rep", "fsdp", None),) * 2 + (placed,) * 4,
        out_specs=(P("fsdp", None),) * 2 + (placed,) * 4,
        check_vma=False,
    )
```

```python
import functools
import math

import jax
import jax.numpy as jnp
from jax import lax
from jax.experimental import pallas as pl
from jax.experimental.pallas import tpu as pltpu
from jax.sharding import PartitionSpec as P

MESH = pl.DeviceIdType.MESH
BF16, F32 = jnp.bfloat16, jnp.float32
LIMIT = 0.25 * math.sqrt(2.0 * 8192 * 4096)
FIRST_Z = 9 / 16
STEP = 16


class Part:
    def __init__(self, rows, columns, sign):
        self.rows, self.columns, self.sign = rows, columns, sign
        self.a = int(rows * FIRST_Z) // STEP * STEP
        self.b = rows - self.a

    def window(self, owner):
        return pl.ds(pl.multiple_of(owner * self.columns, self.columns), self.columns)


def over_rows(rows, body, carry=None):
    def step(i, carry):
        return body(pl.ds(pl.multiple_of(i * STEP, STEP), STEP), carry)

    return lax.fori_loop(0, rows // STEP, step, carry, unroll=2 if rows // STEP % 2 == 0 else 1)


def add_up(out, *terms):
    def body(rows, _):
        total = terms[0][rows, :].astype(F32)
        for term in terms[1:]:
            total = total + term[rows, :].astype(F32)
        out[rows, :] = total.astype(out.dtype)

    over_rows(out.shape[0], body)


def add_up_squares(out, *terms):
    def body(rows, squares):
        total = terms[0][rows, :].astype(F32)
        for term in terms[1:]:
            total = total + term[rows, :].astype(F32)
        out[rows, :] = total
        return squares + total * total

    columns = out.shape[1]
    squares = over_rows(out.shape[0], body, jnp.zeros((STEP, columns), F32))
    line = jnp.sum(squares, axis=0, keepdims=True)
    return functools.reduce(jnp.add, [line[:, k : k + 128] for k in range(0, columns, 128)])


def kernel(parts, *refs):
    delta, master, moment = refs[0:2], refs[2:4], refs[4:6]
    weights, master_next, moment_next = refs[6:8], refs[8:10], refs[10:12]
    at = 12
    bufs = []
    for p in parts:
        names = list(shapes(p))
        bufs.append(dict(zip(names, refs[at : at + len(names)])))
        at += len(names)
    line1, line2, send_sem, recv_sem, local_sem = refs[at:]

    rep, shard = lax.axis_index("rep"), lax.axis_index("fsdp")
    y_hi, z = rep // 4, lax.rem(rep, 4)
    x, y_lo, core = shard // 4, lax.rem(shard // 2, 2), lax.rem(shard, 2)

    def owner(across, dz):
        return (1 - y_hi if across else y_hi) * 4 + lax.rem(z + dz % 4, 4)

    def chip(dx=0, dy=0, dz=0, dc=0):
        y = lax.rem(y_hi * 2 + y_lo + dy, 4)
        there = lax.rem(x + dx, 4) * 4 + lax.rem(y, 2) * 2 + lax.rem(core + dc, 2)
        return (y // 2) * 4 + lax.rem(z + dz, 4), there

    flying, local = {}, []

    def send(key, src, dst, target):
        k = len(flying)
        flying[key] = pltpu.make_async_remote_copy(
            src, dst, send_sem.at[k], recv_sem.at[k], device_id=target, device_id_type=MESH
        )
        flying[key].start()

    def arrived(*key):
        flying[key].wait_recv()

    def along_z(key, src, dst, dz):
        send(key, src, dst, (owner(0, dz), shard))

    def along_y(key, src, dst):
        send(key, src, dst, (owner(1, 0), shard))

    def start_local(src, dst):
        copy = pltpu.make_async_copy(src, dst, local_sem.at[len(local)])
        copy.start()
        local.append(copy)
        return copy

    both = range(len(parts))
    rows_a = [pl.ds(0, p.a) for p in parts]
    rows_b = [pl.ds(p.a, p.b) for p in parts]
    s = [p.sign for p in parts]

    own_a, own_b, params = {}, {}, []
    for side in (0, 1):
        for j in (0, 1):
            for t in both:
                cut = delta[t].at[rows_a[t], parts[t].window(owner(1 - side, (1 - j) * s[t]))]
                own_a[t, j, side] = start_local(cut, bufs[t]["own_a"].at[j, side])
    for k in range(4):
        for t in both:
            cut = delta[t].at[rows_b[t], parts[t].window(owner(0, k * s[t]))]
            own_b[t, k] = start_local(cut, bufs[t]["own_b"].at[k])
    for t in both:
        params.append(start_local(master[t], master_next[t]))
        params.append(start_local(moment[t], moment_next[t]))

    plane = [(dy, dz) for dy in range(4) for dz in range(4)][1:]
    across = [(dx, dc) for dx in range(4) for dc in range(2)][1:]
    barrier = pltpu.get_barrier_semaphore()
    for dy, dz in plane:
        pl.semaphore_signal(barrier, inc=1, device_id=chip(dy=dy, dz=dz), device_id_type=MESH)
    for dx, dc in across:
        pl.semaphore_signal(barrier, inc=1, device_id=chip(dx=dx, dc=dc), device_id_type=MESH)
    pl.semaphore_wait(barrier, len(plane) + len(across))

    def raw_a(side, t):
        p, b = parts[t], bufs[t]
        src = delta[t].at[rows_a[t], p.window(owner(1 - side, 2))]
        along_z(("a2", side, t), src, b["a2"].at[side], s[t])

    def raw_a_alone(side, t):
        p, b = parts[t], bufs[t]
        src = delta[t].at[rows_a[t], p.window(owner(1 - side, -s[t]))]
        along_z(("a1", side, t), src, b["a1"].at[side], -s[t])

    def merge_a(side, t):
        b = bufs[t]
        arrived("a2", side, t)
        own_a[t, 0, side].wait()
        add_up(b["merged_a"].at[side], b["own_a"].at[0, side], b["a2"].at[side])
        along_z(("am", side, t), b["merged_a"].at[side], b["am"].at[side], s[t])

    def raw_b(k, t):
        p, b = parts[t], bufs[t]
        src = delta[t].at[rows_b[t], p.window(owner(1, k * s[t]))]
        along_y(("by", k, t), src, b["by"].at[k])

    for t in both:
        raw_a(0, t)
    for t in both:
        raw_b(2, t)
    for t in both:
        raw_a_alone(0, t)
    for k in (3, 1):
        for t in both:
            raw_b(k, t)
    for t in both:
        merge_a(0, t)
    for t in both:
        raw_a(1, t)
    for t in both:
        raw_a_alone(1, t)
    for t in both:
        b = bufs[t]
        arrived("by", 2, t)
        own_b[t, 2].wait()
        add_up(b["sum_b"].at[0], b["own_b"].at[2], b["by"].at[2])
        along_z(("b2", t), b["sum_b"].at[0], b["b2"], s[t])
    for t in both:
        b = bufs[t]
        arrived("by", 3, t)
        own_b[t, 3].wait()
        add_up(b["sum_b"].at[1], b["own_b"].at[3], b["by"].at[3])
        along_z(("b1", t), b["sum_b"].at[1], b["b1"], -s[t])
    for t in both:
        b = bufs[t]
        arrived("a1", 0, t)
        arrived("am", 0, t)
        own_a[t, 1, 0].wait()
        add_up(b["sum_a"], b["own_a"].at[1, 0], b["a1"].at[0], b["am"].at[0])
        along_y(("ay", t), b["sum_a"], b["ay"])
    for t in both:
        raw_b(0, t)
    for t in both:
        merge_a(1, t)
    for t in both:
        b = bufs[t]
        arrived("by", 1, t)
        arrived("b2", t)
        own_b[t, 1].wait()
        add_up(b["sum_b"].at[2], b["own_b"].at[1], b["by"].at[1], b["b2"])
        along_z(("bm", t), b["sum_b"].at[2], b["bm"], s[t])

    for copy in params:
        copy.wait()
    for t in both:

        def base(rows, _, t=t):
            master_next[t][rows, :] = master_next[t][rows, :] - 0.567 * moment_next[t][rows, :]

        over_rows(parts[t].rows, base)

    line = jnp.zeros((1, 128), F32)
    for t in both:
        b, p = bufs[t], parts[t]
        arrived("a1", 1, t)
        arrived("am", 1, t)
        arrived("ay", t)
        own_a[t, 1, 1].wait()
        terms = (b["own_a"].at[1, 1], b["a1"].at[1], b["am"].at[1], b["ay"])
        line += add_up_squares(b["total"].at[rows_a[t]], *terms)
    for t in both:
        b, p = bufs[t], parts[t]
        arrived("by", 0, t)
        arrived("b1", t)
        arrived("bm", t)
        own_b[t, 0].wait()
        terms = (b["own_b"].at[0], b["by"].at[0], b["b1"], b["bm"])
        line += add_up_squares(b["total"].at[rows_b[t]], *terms)

    line1[pl.ds(0, 1)] = line
    for i, (dy, dz) in enumerate(plane):
        send(("n1", i), line1.at[pl.ds(0, 1)], line1.at[pl.ds(i + 1, 1)], chip(dy=dy, dz=dz))
    for i in range(len(plane)):
        arrived("n1", i)
    line2[pl.ds(0, 1)] = jnp.sum(line1[...], axis=0, keepdims=True)
    for i, (dx, dc) in enumerate(across):
        send(("n2", i), line2.at[pl.ds(0, 1)], line2.at[pl.ds(i + 1, 1)], chip(dx=dx, dc=dc))
    for i in range(len(across)):
        arrived("n2", i)
    square_sum = jnp.sum(line2[...], axis=(0, 1), keepdims=True) * (1.0 / 64.0)
    factor = jnp.minimum(1.0, LIMIT / jnp.sqrt(square_sum + 1e-06)) * 0.125

    def update(t, first, rows_here):
        b = bufs[t]
        scale = 1.33 * factor
        mine = parts[t].window(rep)

        def body(rows, _):
            rows = pl.ds(pl.multiple_of(first + rows.start, STEP), STEP)
            new = master_next[t][rows, :] - scale * b["total"][rows, :]
            master_next[t][rows, :] = new
            weights[t][rows, mine] = new.astype(BF16)

        over_rows(rows_here, body)

    def out_at(t, rows, who):
        return weights[t].at[rows, parts[t].window(who)]

    def give(t, rows, dz, who):
        key = ("w", t, rows is rows_a[t], dz, who)
        place = out_at(t, rows, owner(*who))
        if dz is None:
            along_y(key, place, place)
        else:
            along_z(key, place, place, dz)

    def got(t, rows, dz, who):
        arrived("w", t, rows is rows_a[t], dz, who)

    own = (0, 0)
    for t in both:
        update(t, 0, parts[t].a)
        give(t, rows_a[t], None, own)
    for t in both:
        update(t, parts[t].a, parts[t].b)
        for dz in (s[t], -s[t]):
            give(t, rows_b[t], dz, own)
    for t in both:
        give(t, rows_b[t], None, own)
    for t in both:
        for dz in (s[t], -s[t]):
            give(t, rows_a[t], dz, own)

    def next_moment(t):
        b, m = bufs[t], moment_next[t]

        def body(rows, _):
            m[rows, :] = 0.9 * m[rows, :] + factor * b["total"][rows, :]

        over_rows(parts[t].rows, body)

    for t in both:
        got(t, rows_b[t], s[t], own)
        give(t, rows_b[t], s[t], (0, -s[t]))
        give(t, rows_b[t], None, (0, -s[t]))
    for t in both:
        got(t, rows_b[t], -s[t], own)
        give(t, rows_b[t], None, (0, s[t]))
    for t in both:
        next_moment(t)
    for t in both:
        got(t, rows_a[t], None, own)
        for dz in (s[t], -s[t]):
            give(t, rows_a[t], dz, (1, 0))
    for t in both:
        got(t, rows_b[t], s[t], (0, -s[t]))
        give(t, rows_b[t], None, (0, 2))
    for t in both:
        got(t, rows_a[t], s[t], own)
        give(t, rows_a[t], s[t], (0, -s[t]))
    for t in both:
        got(t, rows_a[t], s[t], (1, 0))
        give(t, rows_a[t], s[t], (1, -s[t]))
    for t in both:
        got(t, rows_a[t], -s[t], own)
        got(t, rows_a[t], -s[t], (1, 0))
        got(t, rows_a[t], s[t], (0, -s[t]))
        got(t, rows_a[t], s[t], (1, -s[t]))
        for who in (own, (0, -s[t]), (0, s[t]), (0, 2)):
            got(t, rows_b[t], None, who)
    for copy in flying.values():
        copy.wait_send()


def shapes(p):
    a, b, c = p.a, p.b, p.columns
    return {
        "own_a": (2, 2, a, c),
        "own_b": (4, b, c),
        "a2": (2, a, c),
        "a1": (2, a, c),
        "am": (2, a, c),
        "ay": (a, c),
        "merged_a": (2, a, c),
        "sum_a": (a, c),
        "by": (4, b, c),
        "b2": (b, c),
        "b1": (b, c),
        "bm": (b, c),
        "sum_b": (3, b, c),
        "total": (p.rows, c),
    }


def scratch(p):
    return [pltpu.VMEM(shape, F32 if n == "total" else BF16) for n, shape in shapes(p).items()]


def write_out(*refs):
    count = len(refs) // 2
    copies = [pltpu.make_async_copy(refs[i], refs[count + i], refs[-1].at[i]) for i in range(count)]
    for copy in copies:
        copy.start()
    for copy in copies:
        copy.wait()


def on_device(delta_query, delta_output, *params):
    deltas = (delta_query[0], delta_output[0])
    parts = (Part(*params[0].shape, 1), Part(*params[1].shape, -1))
    outs = [(d.shape, BF16) for d in deltas] + [(p.shape, F32) for p in params]
    in_hbm = pl.BlockSpec(memory_space=pltpu.HBM)
    in_vmem = pl.BlockSpec(memory_space=pltpu.VMEM)
    held = pl.pallas_call(
        functools.partial(kernel, parts),
        out_shape=[pltpu.VMEM(*out) for out in outs],
        in_specs=[in_hbm] * 6,
        out_specs=[in_vmem] * 6,
        scratch_shapes=[
            *scratch(parts[0]),
            *scratch(parts[1]),
            pltpu.VMEM((16, 128), F32),
            pltpu.VMEM((8, 128), F32),
            pltpu.SemaphoreType.DMA((80,)),
            pltpu.SemaphoreType.DMA((80,)),
            pltpu.SemaphoreType.DMA((32,)),
        ],
        compiler_params=pltpu.CompilerParams(
            collective_id=0, has_side_effects=True, vmem_limit_bytes=44 << 20
        ),
        name="outer_step",
    )(*deltas, *params)
    return pl.pallas_call(
        write_out,
        out_shape=[jax.ShapeDtypeStruct(*out) for out in outs],
        in_specs=[in_vmem] * 6,
        out_specs=[in_hbm] * 6,
        scratch_shapes=[pltpu.SemaphoreType.DMA((6,))],
        compiler_params=pltpu.CompilerParams(vmem_limit_bytes=16 << 20),
        name="write_out",
    )(*held)


def solution(mesh):
    placed = P("fsdp", "rep")
    return jax.shard_map(
        on_device,
        mesh=mesh,
        in_specs=(P("rep", "fsdp", None),) * 2 + (placed,) * 4,
        out_specs=(P("fsdp", None),) * 2 + (placed,) * 4,
        check_vma=False,
    )
```

```python
import functools
import math

import jax
import jax.numpy as jnp
from jax import lax
from jax.experimental import pallas as pl
from jax.experimental.pallas import tpu as pltpu
from jax.sharding import PartitionSpec as P

MESH = pl.DeviceIdType.MESH
BF16, F32 = jnp.bfloat16, jnp.float32
LIMIT = 0.25 * math.sqrt(2.0 * 8192 * 4096)
FIRST_Z = 9 / 16
EARLY = 3 / 16
STEP = 16


class Part:
    def __init__(self, rows, columns, sign):
        self.rows, self.columns, self.sign = rows, columns, sign
        self.a = int(rows * FIRST_Z) // STEP * STEP
        self.b = rows - self.a
        self.g = int(rows * EARLY) // STEP * STEP

    def window(self, owner):
        return pl.ds(pl.multiple_of(owner * self.columns, self.columns), self.columns)


def over_rows(rows, body, carry=None):
    def step(i, carry):
        return body(pl.ds(pl.multiple_of(i * STEP, STEP), STEP), carry)

    return lax.fori_loop(0, rows // STEP, step, carry, unroll=2 if rows // STEP % 2 == 0 else 1)


def add_up(out, *terms):
    def body(rows, _):
        total = terms[0][rows, :].astype(F32)
        for term in terms[1:]:
            total = total + term[rows, :].astype(F32)
        out[rows, :] = total.astype(out.dtype)

    over_rows(out.shape[0], body)


def add_up_squares(out, *terms):
    def body(rows, squares):
        total = terms[0][rows, :].astype(F32)
        for term in terms[1:]:
            total = total + term[rows, :].astype(F32)
        out[rows, :] = total
        return squares + total * total

    columns = out.shape[1]
    squares = over_rows(out.shape[0], body, jnp.zeros((STEP, columns), F32))
    line = jnp.sum(squares, axis=0, keepdims=True)
    return functools.reduce(jnp.add, [line[:, k : k + 128] for k in range(0, columns, 128)])


def kernel(parts, *refs):
    delta, master, moment = refs[0:2], refs[2:4], refs[4:6]
    weights, master_next, moment_next = refs[6:8], refs[8:10], refs[10:12]
    at = 12
    bufs = []
    for p in parts:
        names = list(shapes(p))
        bufs.append(dict(zip(names, refs[at : at + len(names)])))
        at += len(names)
    line1, line2, send_sem, recv_sem, local_sem = refs[at:]

    rep, shard = lax.axis_index("rep"), lax.axis_index("fsdp")
    y_hi, z = rep // 4, lax.rem(rep, 4)
    x, y_lo, core = shard // 4, lax.rem(shard // 2, 2), lax.rem(shard, 2)

    def owner(across, dz):
        return (1 - y_hi if across else y_hi) * 4 + lax.rem(z + dz % 4, 4)

    def chip(dx=0, dy=0, dz=0, dc=0):
        y = lax.rem(y_hi * 2 + y_lo + dy, 4)
        there = lax.rem(x + dx, 4) * 4 + lax.rem(y, 2) * 2 + lax.rem(core + dc, 2)
        return (y // 2) * 4 + lax.rem(z + dz, 4), there

    flying, local = {}, []

    def send(key, src, dst, target):
        k = len(flying)
        flying[key] = pltpu.make_async_remote_copy(
            src, dst, send_sem.at[k], recv_sem.at[k], device_id=target, device_id_type=MESH
        )
        flying[key].start()

    def arrived(*key):
        flying[key].wait_recv()

    def along_z(key, src, dst, dz):
        send(key, src, dst, (owner(0, dz), shard))

    def along_y(key, src, dst):
        send(key, src, dst, (owner(1, 0), shard))

    def start_local(src, dst):
        copy = pltpu.make_async_copy(src, dst, local_sem.at[len(local)])
        copy.start()
        local.append(copy)
        return copy

    both = range(len(parts))
    rows_a = [pl.ds(0, p.a) for p in parts]
    rows_b = [pl.ds(p.a, p.b) for p in parts]
    rows_g = [pl.ds(0, p.g) for p in parts]
    rows_h = [pl.ds(p.g, p.a - p.g) for p in parts]
    s = [p.sign for p in parts]

    plane = [(dy, dz) for dy in range(4) for dz in range(4)][1:]
    across = [(dx, dc) for dx in range(4) for dc in range(2)][1:]
    barrier = pltpu.get_barrier_semaphore()
    for dy, dz in plane:
        pl.semaphore_signal(barrier, inc=1, device_id=chip(dy=dy, dz=dz), device_id_type=MESH)
    for dx, dc in across:
        pl.semaphore_signal(barrier, inc=1, device_id=chip(dx=dx, dc=dc), device_id_type=MESH)
    pl.semaphore_wait(barrier, len(plane) + len(across))

    def raw_a(side, t):
        p, b = parts[t], bufs[t]
        src = delta[t].at[rows_a[t], p.window(owner(1 - side, 2))]
        along_z(("a2", side, t), src, b["a2"].at[side], s[t])

    def raw_a_alone(side, t):
        p, b = parts[t], bufs[t]
        src = delta[t].at[rows_a[t], p.window(owner(1 - side, -s[t]))]
        along_z(("a1", side, t), src, b["a1"].at[side], -s[t])

    def merge_a(side, t):
        b = bufs[t]
        arrived("a2", side, t)
        own_a[t, 0, side].wait()
        add_up(b["merged_a"].at[side], b["own_a"].at[0, side], b["a2"].at[side])
        along_z(("am", side, t), b["merged_a"].at[side], b["am"].at[side], s[t])

    def raw_b(k, t):
        p, b = parts[t], bufs[t]
        src = delta[t].at[rows_b[t], p.window(owner(1, k * s[t]))]
        along_y(("by", k, t), src, b["by"].at[k])

    for t in both:
        raw_a(0, t)
    for t in both:
        raw_b(2, t)
    for t in both:
        raw_a_alone(0, t)
    for k in (3, 1):
        for t in both:
            raw_b(k, t)

    own_a, own_b, params = {}, {}, []
    for side in (0, 1):
        for j in (0, 1):
            for t in both:
                cut = delta[t].at[rows_a[t], parts[t].window(owner(1 - side, (1 - j) * s[t]))]
                own_a[t, j, side] = start_local(cut, bufs[t]["own_a"].at[j, side])
    for k in range(4):
        for t in both:
            cut = delta[t].at[rows_b[t], parts[t].window(owner(0, k * s[t]))]
            own_b[t, k] = start_local(cut, bufs[t]["own_b"].at[k])
    for t in both:
        params.append(start_local(master[t], master_next[t]))
        params.append(start_local(moment[t], moment_next[t]))

    for t in both:
        merge_a(0, t)
    for t in both:
        raw_a(1, t)
    for t in both:
        raw_a_alone(1, t)
    for t in both:
        b = bufs[t]
        arrived("by", 2, t)
        own_b[t, 2].wait()
        add_up(b["sum_b"].at[0], b["own_b"].at[2], b["by"].at[2])
        along_z(("b2", t), b["sum_b"].at[0], b["b2"], s[t])
    for t in both:
        b = bufs[t]
        arrived("by", 3, t)
        own_b[t, 3].wait()
        add_up(b["sum_b"].at[1], b["own_b"].at[3], b["by"].at[3])
        along_z(("b1", t), b["sum_b"].at[1], b["b1"], -s[t])
    for t in both:
        b = bufs[t]
        arrived("a1", 0, t)
        arrived("am", 0, t)
        own_a[t, 1, 0].wait()
        add_up(b["sum_a"], b["own_a"].at[1, 0], b["a1"].at[0], b["am"].at[0])
        along_y(("ay", t), b["sum_a"], b["ay"])
    for t in both:
        raw_b(0, t)
    for t in both:
        merge_a(1, t)
    for t in both:
        b = bufs[t]
        arrived("by", 1, t)
        arrived("b2", t)
        own_b[t, 1].wait()
        add_up(b["sum_b"].at[2], b["own_b"].at[1], b["by"].at[1], b["b2"])
        along_z(("bm", t), b["sum_b"].at[2], b["bm"], s[t])

    for copy in params:
        copy.wait()
    for t in both:

        def base(rows, _, t=t):
            master_next[t][rows, :] = master_next[t][rows, :] - 0.567 * moment_next[t][rows, :]

        over_rows(parts[t].rows, base)

    def early(name, t):
        b = bufs[t]
        for slot, dz in enumerate((s[t], -s[t])):
            along_z((name, slot, t), b[name], b["got_" + name].at[slot], dz)
        along_y((name, 2, t), b[name], b["got_" + name].at[2])

    for t in both:
        add_up(bufs[t]["u"], master_next[t])
    for t in both:
        early("u", t)

    line = jnp.zeros((1, 128), F32)
    for t in both:
        b, p = bufs[t], parts[t]
        arrived("a1", 1, t)
        arrived("am", 1, t)
        arrived("ay", t)
        own_a[t, 1, 1].wait()
        terms = (b["own_a"].at[1, 1], b["a1"].at[1], b["am"].at[1], b["ay"])
        line += add_up_squares(b["total"].at[rows_a[t]], *terms)
    for t in both:
        b, p = bufs[t], parts[t]
        arrived("by", 0, t)
        arrived("b1", t)
        arrived("bm", t)
        own_b[t, 0].wait()
        terms = (b["own_b"].at[0], b["by"].at[0], b["b1"], b["bm"])
        line += add_up_squares(b["total"].at[rows_b[t]], *terms)

    line1[pl.ds(0, 1)] = line
    for i, (dy, dz) in enumerate(plane):
        send(("n1", i), line1.at[pl.ds(0, 1)], line1.at[pl.ds(i + 1, 1)], chip(dy=dy, dz=dz))
    for t in both:
        add_up(bufs[t]["v"], bufs[t]["total"])
    for t in both:
        early("v", t)
    for i in range(len(plane)):
        arrived("n1", i)
    line2[pl.ds(0, 1)] = jnp.sum(line1[...], axis=0, keepdims=True)
    for i, (dx, dc) in enumerate(across):
        send(("n2", i), line2.at[pl.ds(0, 1)], line2.at[pl.ds(i + 1, 1)], chip(dx=dx, dc=dc))
    for i in range(len(across)):
        arrived("n2", i)
    square_sum = jnp.sum(line2[...], axis=(0, 1), keepdims=True) * (1.0 / 64.0)
    factor = jnp.minimum(1.0, LIMIT / jnp.sqrt(square_sum + 1e-06)) * 0.125

    scale = 1.33 * factor

    def update(t, first, count, weights_too):
        b = bufs[t]
        mine = parts[t].window(rep)

        def body(rows, _):
            rows = pl.ds(pl.multiple_of(first + rows.start, STEP), STEP)
            new = master_next[t][rows, :] - scale * b["total"][rows, :]
            master_next[t][rows, :] = new
            if weights_too:
                weights[t][rows, mine] = new.astype(BF16)

        over_rows(count, body)

    def next_moment(t):
        b, m = bufs[t], moment_next[t]

        def body(rows, _):
            m[rows, :] = 0.9 * m[rows, :] + factor * b["total"][rows, :]

        over_rows(parts[t].rows, body)

    def work_out(t, u, v, who):
        columns = parts[t].window(owner(*who))

        def body(rows, _):
            new = u[rows, :].astype(F32) - scale * v[rows, :].astype(F32)
            weights[t][rows, columns] = new.astype(BF16)

        over_rows(parts[t].g, body)

    def work_out_got(t, slot, who):
        arrived("u", slot, t)
        arrived("v", slot, t)
        work_out(t, bufs[t]["got_u"].at[slot], bufs[t]["got_v"].at[slot], who)

    def give(t, rows, dz, who):
        place = weights[t].at[rows, parts[t].window(owner(*who))]
        key = ("w", t, rows.start, rows.size, dz, who)
        if dz is None:
            along_y(key, place, place)
        else:
            along_z(key, place, place, dz)

    def got(t, rows, dz, who):
        arrived("w", t, rows.start, rows.size, dz, who)

    own = (0, 0)
    for t in both:
        update(t, parts[t].g, parts[t].a - parts[t].g, True)
        give(t, rows_h[t], None, own)
    for t in both:
        update(t, parts[t].a, parts[t].b, True)
        for dz in (s[t], -s[t]):
            give(t, rows_b[t], dz, own)
    for t in both:
        give(t, rows_b[t], None, own)
    for t in both:
        for dz in (s[t], -s[t]):
            give(t, rows_h[t], dz, own)
    for t in both:
        work_out_got(t, 0, (0, -s[t]))
        give(t, rows_g[t], s[t], (0, -s[t]))
    for t in both:
        work_out_got(t, 2, (1, 0))
        for dz in (s[t], -s[t]):
            give(t, rows_g[t], dz, (1, 0))

    for t in both:
        got(t, rows_b[t], s[t], own)
        give(t, rows_b[t], s[t], (0, -s[t]))
        give(t, rows_b[t], None, (0, -s[t]))
    for t in both:
        got(t, rows_b[t], -s[t], own)
        give(t, rows_b[t], None, (0, s[t]))
    for t in both:
        got(t, rows_h[t], None, own)
        for dz in (s[t], -s[t]):
            give(t, rows_h[t], dz, (1, 0))
    for t in both:
        got(t, rows_h[t], s[t], own)
        give(t, rows_h[t], s[t], (0, -s[t]))
    for t in both:
        work_out(t, bufs[t]["u"], bufs[t]["v"], own)
        work_out_got(t, 1, (0, s[t]))
    for t in both:
        update(t, 0, parts[t].g, False)
        next_moment(t)
    for t in both:
        got(t, rows_b[t], s[t], (0, -s[t]))
        give(t, rows_b[t], None, (0, 2))
    for t in both:
        got(t, rows_g[t], s[t], (1, 0))
        got(t, rows_h[t], s[t], (1, 0))
        give(t, rows_a[t], s[t], (1, -s[t]))
    for t in both:
        got(t, rows_h[t], -s[t], own)
        got(t, rows_g[t], -s[t], (1, 0))
        got(t, rows_h[t], -s[t], (1, 0))
        got(t, rows_g[t], s[t], (0, -s[t]))
        got(t, rows_h[t], s[t], (0, -s[t]))
        got(t, rows_a[t], s[t], (1, -s[t]))
        for who in (own, (0, -s[t]), (0, s[t]), (0, 2)):
            got(t, rows_b[t], None, who)
    for copy in flying.values():
        copy.wait_send()


def shapes(p):
    a, b, g, c = p.a, p.b, p.g, p.columns
    return {
        "own_a": (2, 2, a, c),
        "own_b": (4, b, c),
        "a2": (2, a, c),
        "a1": (2, a, c),
        "am": (2, a, c),
        "ay": (a, c),
        "merged_a": (2, a, c),
        "sum_a": (a, c),
        "by": (4, b, c),
        "b2": (b, c),
        "b1": (b, c),
        "bm": (b, c),
        "sum_b": (3, b, c),
        "u": (g, c),
        "v": (g, c),
        "got_u": (3, g, c),
        "got_v": (3, g, c),
        "total": (p.rows, c),
    }


def scratch(p):
    return [pltpu.VMEM(shape, F32 if n == "total" else BF16) for n, shape in shapes(p).items()]


def write_out(*refs):
    count = len(refs) // 2
    copies = [pltpu.make_async_copy(refs[i], refs[count + i], refs[-1].at[i]) for i in range(count)]
    for copy in copies:
        copy.start()
    for copy in copies:
        copy.wait()


def on_device(delta_query, delta_output, *params):
    deltas = (delta_query[0], delta_output[0])
    parts = (Part(*params[0].shape, 1), Part(*params[1].shape, -1))
    outs = [(d.shape, BF16) for d in deltas] + [(p.shape, F32) for p in params]
    in_hbm = pl.BlockSpec(memory_space=pltpu.HBM)
    in_vmem = pl.BlockSpec(memory_space=pltpu.VMEM)
    held = pl.pallas_call(
        functools.partial(kernel, parts),
        out_shape=[pltpu.VMEM(*out) for out in outs],
        in_specs=[in_hbm] * 6,
        out_specs=[in_vmem] * 6,
        scratch_shapes=[
            *scratch(parts[0]),
            *scratch(parts[1]),
            pltpu.VMEM((16, 128), F32),
            pltpu.VMEM((8, 128), F32),
            pltpu.SemaphoreType.DMA((104,)),
            pltpu.SemaphoreType.DMA((104,)),
            pltpu.SemaphoreType.DMA((32,)),
        ],
        compiler_params=pltpu.CompilerParams(
            collective_id=0, has_side_effects=True, vmem_limit_bytes=44 << 20
        ),
        name="outer_step",
    )(*deltas, *params)
    return pl.pallas_call(
        write_out,
        out_shape=[jax.ShapeDtypeStruct(*out) for out in outs],
        in_specs=[in_vmem] * 6,
        out_specs=[in_hbm] * 6,
        scratch_shapes=[pltpu.SemaphoreType.DMA((6,))],
        compiler_params=pltpu.CompilerParams(vmem_limit_bytes=16 << 20),
        name="write_out",
    )(*held)


def solution(mesh):
    placed = P("fsdp", "rep")
    return jax.shard_map(
        on_device,
        mesh=mesh,
        in_specs=(P("rep", "fsdp", None),) * 2 + (placed,) * 4,
        out_specs=(P("fsdp", None),) * 2 + (placed,) * 4,
        check_vma=False,
    )
```

```python
import functools
import math

import jax
import jax.numpy as jnp
from jax import lax
from jax.experimental import pallas as pl
from jax.experimental.pallas import tpu as pltpu
from jax.sharding import PartitionSpec as P

MESH = pl.DeviceIdType.MESH
BF16, F32 = jnp.bfloat16, jnp.float32
LIMIT = 0.25 * math.sqrt(2.0 * 8192 * 4096)
FIRST_Z = 9 / 16
EARLY = 3 / 16
STEP = 16


class Part:
    def __init__(self, rows, columns, sign):
        self.rows, self.columns, self.sign = rows, columns, sign
        self.a = int(rows * FIRST_Z) // STEP * STEP
        self.b = rows - self.a
        self.g = int(rows * EARLY) // STEP * STEP

    def window(self, owner):
        return pl.ds(pl.multiple_of(owner * self.columns, self.columns), self.columns)


def over_rows(rows, body, carry=None):
    def step(i, carry):
        return body(pl.ds(pl.multiple_of(i * STEP, STEP), STEP), carry)

    return lax.fori_loop(0, rows // STEP, step, carry, unroll=2 if rows // STEP % 2 == 0 else 1)


def add_up(out, *terms):
    def body(rows, _):
        total = terms[0][rows, :].astype(F32)
        for term in terms[1:]:
            total = total + term[rows, :].astype(F32)
        out[rows, :] = total.astype(out.dtype)

    over_rows(out.shape[0], body)


def add_up_squares(out, *terms):
    def body(rows, squares):
        total = terms[0][rows, :].astype(F32)
        for term in terms[1:]:
            total = total + term[rows, :].astype(F32)
        out[rows, :] = total
        return squares + total * total

    columns = out.shape[1]
    squares = over_rows(out.shape[0], body, jnp.zeros((STEP, columns), F32))
    line = jnp.sum(squares, axis=0, keepdims=True)
    return functools.reduce(jnp.add, [line[:, k : k + 128] for k in range(0, columns, 128)])


def kernel(parts, *refs):
    delta, master, moment = refs[0:2], refs[2:4], refs[4:6]
    weights, master_next, moment_next = refs[6:8], refs[8:10], refs[10:12]
    at = 12
    bufs = []
    for p in parts:
        names = list(shapes(p))
        bufs.append(dict(zip(names, refs[at : at + len(names)])))
        at += len(names)
    line1, line2, links, send_sem, recv_sem, local_sem = refs[at:]

    rep, shard = lax.axis_index("rep"), lax.axis_index("fsdp")
    y_hi, z = rep // 4, lax.rem(rep, 4)
    x, y_lo, core = shard // 4, lax.rem(shard // 2, 2), lax.rem(shard, 2)

    def owner(across, dz):
        return (1 - y_hi if across else y_hi) * 4 + lax.rem(z + dz % 4, 4)

    def chip(dx=0, dy=0, dz=0, dc=0):
        y = lax.rem(y_hi * 2 + y_lo + dy, 4)
        there = lax.rem(x + dx, 4) * 4 + lax.rem(y, 2) * 2 + lax.rem(core + dc, 2)
        return (y // 2) * 4 + lax.rem(z + dz, 4), there

    flying, local = {}, []

    def send(key, src, dst, target):
        k = len(flying)
        flying[key] = pltpu.make_async_remote_copy(
            src, dst, send_sem.at[k], recv_sem.at[k], device_id=target, device_id_type=MESH
        )
        flying[key].start()

    def arrived(*key):
        flying[key].wait_recv()

    def along_z(key, src, dst, dz):
        send(key, src, dst, (owner(0, dz), shard))

    def along_y(key, src, dst):
        send(key, src, dst, (owner(1, 0), shard))

    def start_local(src, dst):
        copy = pltpu.make_async_copy(src, dst, local_sem.at[len(local)])
        copy.start()
        local.append(copy)
        return copy

    both = range(len(parts))
    rows_a = [pl.ds(0, p.a) for p in parts]
    rows_b = [pl.ds(p.a, p.b) for p in parts]
    rows_g = [pl.ds(0, p.g) for p in parts]
    rows_h = [pl.ds(p.g, p.a - p.g) for p in parts]
    s = [p.sign for p in parts]

    around = {"x": (chip(dx=1), chip(dx=3)), "y": (chip(dy=1), chip(dy=3)), "z": (chip(dz=1), chip(dz=3))}
    near = [*around["z"], chip(dy=2), chip(dc=1), *around["y"], *around["x"]]
    barrier = pltpu.get_barrier_semaphore()
    for target in near:
        pl.semaphore_signal(barrier, inc=1, device_id=target, device_id_type=MESH)
    pl.semaphore_wait(barrier, len(near))

    def tell(i):
        for target in around["xyyzz"[i]]:
            pl.semaphore_signal(links.at[i], inc=1, device_id=target, device_id_type=MESH)

    def told(i):
        pl.semaphore_wait(links.at[i], 2)

    def raw_a(side, t):
        p, b = parts[t], bufs[t]
        src = delta[t].at[rows_a[t], p.window(owner(1 - side, 2))]
        along_z(("a2", side, t), src, b["a2"].at[side], s[t])

    def raw_a_alone(side, t):
        p, b = parts[t], bufs[t]
        src = delta[t].at[rows_a[t], p.window(owner(1 - side, -s[t]))]
        along_z(("a1", side, t), src, b["a1"].at[side], -s[t])

    def merge_a(side, t):
        b = bufs[t]
        arrived("a2", side, t)
        own_a[t, 0, side].wait()
        add_up(b["merged_a"].at[side], b["own_a"].at[0, side], b["a2"].at[side])
        along_z(("am", side, t), b["merged_a"].at[side], b["am"].at[side], s[t])

    def raw_b(k, t):
        p, b = parts[t], bufs[t]
        src = delta[t].at[rows_b[t], p.window(owner(1, k * s[t]))]
        along_y(("by", k, t), src, b["by"].at[k])

    for t in both:
        raw_a(0, t)
    for t in both:
        raw_b(2, t)
    for t in both:
        raw_a_alone(0, t)
    for k in (3, 1):
        for t in both:
            raw_b(k, t)

    own_a, own_b, params = {}, {}, []
    for side in (0, 1):
        for j in (0, 1):
            for t in both:
                cut = delta[t].at[rows_a[t], parts[t].window(owner(1 - side, (1 - j) * s[t]))]
                own_a[t, j, side] = start_local(cut, bufs[t]["own_a"].at[j, side])
    for k in range(4):
        for t in both:
            cut = delta[t].at[rows_b[t], parts[t].window(owner(0, k * s[t]))]
            own_b[t, k] = start_local(cut, bufs[t]["own_b"].at[k])
    for t in both:
        params.append(start_local(master[t], master_next[t]))
        params.append(start_local(moment[t], moment_next[t]))

    tell(0)
    for t in both:
        merge_a(0, t)
    told(0)
    tell(1)
    for t in both:
        raw_a(1, t)
    for t in both:
        raw_a_alone(1, t)
    for t in both:
        b = bufs[t]
        arrived("by", 2, t)
        own_b[t, 2].wait()
        add_up(b["sum_b"].at[0], b["own_b"].at[2], b["by"].at[2])
        along_z(("b2", t), b["sum_b"].at[0], b["b2"], s[t])
    told(1)
    tell(2)
    for t in both:
        b = bufs[t]
        arrived("by", 3, t)
        own_b[t, 3].wait()
        add_up(b["sum_b"].at[1], b["own_b"].at[3], b["by"].at[3])
        along_z(("b1", t), b["sum_b"].at[1], b["b1"], -s[t])
    told(2)
    tell(3)
    for t in both:
        b = bufs[t]
        arrived("a1", 0, t)
        arrived("am", 0, t)
        own_a[t, 1, 0].wait()
        add_up(b["sum_a"], b["own_a"].at[1, 0], b["a1"].at[0], b["am"].at[0])
        along_y(("ay", t), b["sum_a"], b["ay"])
    for t in both:
        raw_b(0, t)
    told(3)
    tell(4)
    for t in both:
        merge_a(1, t)
    told(4)
    for t in both:
        b = bufs[t]
        arrived("by", 1, t)
        arrived("b2", t)
        own_b[t, 1].wait()
        add_up(b["sum_b"].at[2], b["own_b"].at[1], b["by"].at[1], b["b2"])
        along_z(("bm", t), b["sum_b"].at[2], b["bm"], s[t])

    for copy in params:
        copy.wait()
    for t in both:

        def base(rows, _, t=t):
            master_next[t][rows, :] = master_next[t][rows, :] - 0.567 * moment_next[t][rows, :]

        over_rows(parts[t].rows, base)

    def early(name, t):
        b = bufs[t]
        for slot, dz in enumerate((s[t], -s[t])):
            along_z((name, slot, t), b[name], b["got_" + name].at[slot], dz)
        along_y((name, 2, t), b[name], b["got_" + name].at[2])

    for t in both:
        add_up(bufs[t]["u"], master_next[t])
    for t in both:
        early("u", t)

    line = jnp.zeros((1, 128), F32)
    for t in both:
        b, p = bufs[t], parts[t]
        arrived("a1", 1, t)
        arrived("am", 1, t)
        arrived("ay", t)
        own_a[t, 1, 1].wait()
        terms = (b["own_a"].at[1, 1], b["a1"].at[1], b["am"].at[1], b["ay"])
        line += add_up_squares(b["total"].at[rows_a[t]], *terms)
    for t in both:
        b, p = bufs[t], parts[t]
        arrived("by", 0, t)
        arrived("b1", t)
        arrived("bm", t)
        own_b[t, 0].wait()
        terms = (b["own_b"].at[0], b["by"].at[0], b["b1"], b["bm"])
        line += add_up_squares(b["total"].at[rows_b[t]], *terms)

    line1[core] = line
    send(("n1",), line1.at[core], line1.at[core], chip(dc=1))
    arrived("n1")
    here = (x * 4 + y_hi * 2 + y_lo) * 4 + z
    line2[here] = jnp.sum(line1[...], axis=0)
    others = [(dx, dy, dz) for dx in range(4) for dy in range(4) for dz in range(4)][1:]
    for dx, dy, dz in others:
        send(("n2", dx, dy, dz), line2.at[here], line2.at[here], chip(dx=dx, dy=dy, dz=dz))
    for t in both:
        add_up(bufs[t]["v"], bufs[t]["total"])
    for t in both:
        early("v", t)
    for there in others:
        arrived("n2", *there)
    square_sum = jnp.sum(jnp.sum(line2[...], axis=0), axis=1, keepdims=True) * (1.0 / 64.0)
    factor = jnp.minimum(1.0, LIMIT / jnp.sqrt(square_sum + 1e-06)) * 0.125

    scale = 1.33 * factor

    def update(t, first, count, weights_too):
        b = bufs[t]
        mine = parts[t].window(rep)

        def body(rows, _):
            rows = pl.ds(pl.multiple_of(first + rows.start, STEP), STEP)
            new = master_next[t][rows, :] - scale * b["total"][rows, :]
            master_next[t][rows, :] = new
            if weights_too:
                weights[t][rows, mine] = new.astype(BF16)

        over_rows(count, body)

    def next_moment(t):
        b, m = bufs[t], moment_next[t]

        def body(rows, _):
            m[rows, :] = 0.9 * m[rows, :] + factor * b["total"][rows, :]

        over_rows(parts[t].rows, body)

    def work_out(t, u, v, who):
        columns = parts[t].window(owner(*who))

        def body(rows, _):
            new = u[rows, :].astype(F32) - scale * v[rows, :].astype(F32)
            weights[t][rows, columns] = new.astype(BF16)

        over_rows(parts[t].g, body)

    def work_out_got(t, slot, who):
        arrived("u", slot, t)
        arrived("v", slot, t)
        work_out(t, bufs[t]["got_u"].at[slot], bufs[t]["got_v"].at[slot], who)

    def give(t, rows, dz, who):
        place = weights[t].at[rows, parts[t].window(owner(*who))]
        key = ("w", t, rows.start, rows.size, dz, who)
        if dz is None:
            along_y(key, place, place)
        else:
            along_z(key, place, place, dz)

    def got(t, rows, dz, who):
        arrived("w", t, rows.start, rows.size, dz, who)

    own = (0, 0)
    for t in both:
        update(t, parts[t].g, parts[t].a - parts[t].g, True)
        give(t, rows_h[t], None, own)
    for t in both:
        update(t, parts[t].a, parts[t].b, True)
        for dz in (s[t], -s[t]):
            give(t, rows_b[t], dz, own)
    for t in both:
        give(t, rows_b[t], None, own)
    for t in both:
        for dz in (s[t], -s[t]):
            give(t, rows_h[t], dz, own)
    for t in both:
        work_out_got(t, 0, (0, -s[t]))
        give(t, rows_g[t], s[t], (0, -s[t]))
    for t in both:
        work_out_got(t, 2, (1, 0))
        for dz in (s[t], -s[t]):
            give(t, rows_g[t], dz, (1, 0))

    for t in both:
        got(t, rows_b[t], s[t], own)
        give(t, rows_b[t], s[t], (0, -s[t]))
        give(t, rows_b[t], None, (0, -s[t]))
    for t in both:
        got(t, rows_b[t], -s[t], own)
        give(t, rows_b[t], None, (0, s[t]))
    for t in both:
        got(t, rows_h[t], None, own)
        for dz in (s[t], -s[t]):
            give(t, rows_h[t], dz, (1, 0))
    for t in both:
        got(t, rows_h[t], s[t], own)
        give(t, rows_h[t], s[t], (0, -s[t]))
    for t in both:
        work_out(t, bufs[t]["u"], bufs[t]["v"], own)
        work_out_got(t, 1, (0, s[t]))
    for t in both:
        update(t, 0, parts[t].g, False)
        next_moment(t)
    for t in both:
        got(t, rows_b[t], s[t], (0, -s[t]))
        give(t, rows_b[t], None, (0, 2))
    for t in both:
        got(t, rows_g[t], s[t], (1, 0))
        got(t, rows_h[t], s[t], (1, 0))
        give(t, rows_a[t], s[t], (1, -s[t]))
    for t in both:
        got(t, rows_h[t], -s[t], own)
        got(t, rows_g[t], -s[t], (1, 0))
        got(t, rows_h[t], -s[t], (1, 0))
        got(t, rows_g[t], s[t], (0, -s[t]))
        got(t, rows_h[t], s[t], (0, -s[t]))
        got(t, rows_a[t], s[t], (1, -s[t]))
        for who in (own, (0, -s[t]), (0, s[t]), (0, 2)):
            got(t, rows_b[t], None, who)
    for copy in flying.values():
        copy.wait_send()


def shapes(p):
    a, b, g, c = p.a, p.b, p.g, p.columns
    return {
        "own_a": (2, 2, a, c),
        "own_b": (4, b, c),
        "a2": (2, a, c),
        "a1": (2, a, c),
        "am": (2, a, c),
        "ay": (a, c),
        "merged_a": (2, a, c),
        "sum_a": (a, c),
        "by": (4, b, c),
        "b2": (b, c),
        "b1": (b, c),
        "bm": (b, c),
        "sum_b": (3, b, c),
        "u": (g, c),
        "v": (g, c),
        "got_u": (3, g, c),
        "got_v": (3, g, c),
        "total": (p.rows, c),
    }


def scratch(p):
    return [pltpu.VMEM(shape, F32 if n == "total" else BF16) for n, shape in shapes(p).items()]


def write_out(*refs):
    count = len(refs) // 2
    copies = [pltpu.make_async_copy(refs[i], refs[count + i], refs[-1].at[i]) for i in range(count)]
    for copy in copies:
        copy.start()
    for copy in copies:
        copy.wait()


def on_device(delta_query, delta_output, *params):
    deltas = (delta_query[0], delta_output[0])
    parts = (Part(*params[0].shape, 1), Part(*params[1].shape, -1))
    outs = [(d.shape, BF16) for d in deltas] + [(p.shape, F32) for p in params]
    in_hbm = pl.BlockSpec(memory_space=pltpu.HBM)
    in_vmem = pl.BlockSpec(memory_space=pltpu.VMEM)
    held = pl.pallas_call(
        functools.partial(kernel, parts),
        out_shape=[pltpu.VMEM(*out) for out in outs],
        in_specs=[in_hbm] * 6,
        out_specs=[in_vmem] * 6,
        scratch_shapes=[
            *scratch(parts[0]),
            *scratch(parts[1]),
            pltpu.VMEM((2, 1, 128), F32),
            pltpu.VMEM((64, 1, 128), F32),
            pltpu.SemaphoreType.REGULAR((5,)),
            pltpu.SemaphoreType.DMA((144,)),
            pltpu.SemaphoreType.DMA((144,)),
            pltpu.SemaphoreType.DMA((32,)),
        ],
        compiler_params=pltpu.CompilerParams(
            collective_id=0, has_side_effects=True, vmem_limit_bytes=44 << 20
        ),
        name="outer_step",
    )(*deltas, *params)
    return pl.pallas_call(
        write_out,
        out_shape=[jax.ShapeDtypeStruct(*out) for out in outs],
        in_specs=[in_vmem] * 6,
        out_specs=[in_hbm] * 6,
        scratch_shapes=[pltpu.SemaphoreType.DMA((6,))],
        compiler_params=pltpu.CompilerParams(vmem_limit_bytes=16 << 20),
        name="write_out",
    )(*held)


def solution(mesh):
    placed = P("fsdp", "rep")
    return jax.shard_map(
        on_device,
        mesh=mesh,
        in_specs=(P("rep", "fsdp", None),) * 2 + (placed,) * 4,
        out_specs=(P("fsdp", None),) * 2 + (placed,) * 4,
        check_vma=False,
    )
```

```python
import functools
import math

import jax
import jax.numpy as jnp
from jax import lax
from jax.experimental import pallas as pl
from jax.experimental.pallas import tpu as pltpu
from jax.sharding import PartitionSpec as P

MESH = pl.DeviceIdType.MESH
BF16, F32 = jnp.bfloat16, jnp.float32
LIMIT = 0.25 * math.sqrt(2.0 * 8192 * 4096)
FIRST_Z = 9 / 16
EARLY = 1 / 4
STEP = 16


class Part:
    def __init__(self, rows, columns, sign):
        self.rows, self.columns, self.sign = rows, columns, sign
        self.a = int(rows * FIRST_Z) // STEP * STEP
        self.b = rows - self.a
        self.g = int(rows * EARLY) // STEP * STEP

    def window(self, owner):
        return pl.ds(pl.multiple_of(owner * self.columns, self.columns), self.columns)


def over_rows(rows, body, carry=None):
    def step(i, carry):
        return body(pl.ds(pl.multiple_of(i * STEP, STEP), STEP), carry)

    return lax.fori_loop(0, rows // STEP, step, carry, unroll=2 if rows // STEP % 2 == 0 else 1)


def add_up(out, *terms):
    def body(rows, _):
        total = terms[0][rows, :].astype(F32)
        for term in terms[1:]:
            total = total + term[rows, :].astype(F32)
        out[rows, :] = total.astype(out.dtype)

    over_rows(out.shape[0], body)


def add_up_squares(out, *terms):
    def body(rows, squares):
        total = terms[0][rows, :].astype(F32)
        for term in terms[1:]:
            total = total + term[rows, :].astype(F32)
        out[rows, :] = total
        return squares + total * total

    columns = out.shape[1]
    squares = over_rows(out.shape[0], body, jnp.zeros((STEP, columns), F32))
    line = jnp.sum(squares, axis=0, keepdims=True)
    return functools.reduce(jnp.add, [line[:, k : k + 128] for k in range(0, columns, 128)])


def kernel(parts, *refs):
    delta, master, moment = refs[0:2], refs[2:4], refs[4:6]
    weights, master_next, moment_next = refs[6:8], refs[8:10], refs[10:12]
    at = 12
    bufs = []
    for p in parts:
        names = list(shapes(p))
        bufs.append(dict(zip(names, refs[at : at + len(names)])))
        at += len(names)
    line1, line2, links, send_sem, recv_sem, local_sem = refs[at:]

    rep, shard = lax.axis_index("rep"), lax.axis_index("fsdp")
    y_hi, z = rep // 4, lax.rem(rep, 4)
    x, y_lo, core = shard // 4, lax.rem(shard // 2, 2), lax.rem(shard, 2)

    def owner(across, dz):
        return (1 - y_hi if across else y_hi) * 4 + lax.rem(z + dz % 4, 4)

    def chip(dx=0, dy=0, dz=0, dc=0):
        y = lax.rem(y_hi * 2 + y_lo + dy, 4)
        there = lax.rem(x + dx, 4) * 4 + lax.rem(y, 2) * 2 + lax.rem(core + dc, 2)
        return (y // 2) * 4 + lax.rem(z + dz, 4), there

    flying, local = {}, []

    def send(key, src, dst, target):
        k = len(flying)
        flying[key] = pltpu.make_async_remote_copy(
            src, dst, send_sem.at[k], recv_sem.at[k], device_id=target, device_id_type=MESH
        )
        flying[key].start()

    def arrived(*key):
        flying[key].wait_recv()

    def along_z(key, src, dst, dz):
        send(key, src, dst, (owner(0, dz), shard))

    def along_y(key, src, dst):
        send(key, src, dst, (owner(1, 0), shard))

    def start_local(src, dst):
        copy = pltpu.make_async_copy(src, dst, local_sem.at[len(local)])
        copy.start()
        local.append(copy)
        return copy

    both = range(len(parts))
    rows_a = [pl.ds(0, p.a) for p in parts]
    rows_b = [pl.ds(p.a, p.b) for p in parts]
    rows_g = [pl.ds(0, p.g) for p in parts]
    rows_h = [pl.ds(p.g, p.a - p.g) for p in parts]
    s = [p.sign for p in parts]

    around = {"x": (chip(dx=1), chip(dx=3)), "y": (chip(dy=1), chip(dy=3)), "z": (chip(dz=1), chip(dz=3))}
    near = [*around["z"], chip(dy=2), chip(dc=1), *around["y"], *around["x"]]
    barrier = pltpu.get_barrier_semaphore()
    for target in near:
        pl.semaphore_signal(barrier, inc=1, device_id=target, device_id_type=MESH)
    pl.semaphore_wait(barrier, len(near))

    def tell(i):
        for target in around["xyyzz"[i]]:
            pl.semaphore_signal(links.at[i], inc=1, device_id=target, device_id_type=MESH)

    def told(i):
        pl.semaphore_wait(links.at[i], 2)

    def raw_a(side, t):
        p, b = parts[t], bufs[t]
        src = delta[t].at[rows_a[t], p.window(owner(1 - side, 2))]
        along_z(("a2", side, t), src, b["a2"].at[side], s[t])

    def raw_a_alone(side, t):
        p, b = parts[t], bufs[t]
        src = delta[t].at[rows_a[t], p.window(owner(1 - side, -s[t]))]
        along_z(("a1", side, t), src, b["a1"].at[side], -s[t])

    def merge_a(side, t):
        b = bufs[t]
        arrived("a2", side, t)
        own_a[t, 0, side].wait()
        add_up(b["merged_a"].at[side], b["own_a"].at[0, side], b["a2"].at[side])
        along_z(("am", side, t), b["merged_a"].at[side], b["am"].at[side], s[t])

    def raw_b(k, t):
        p, b = parts[t], bufs[t]
        src = delta[t].at[rows_b[t], p.window(owner(1, k * s[t]))]
        along_y(("by", k, t), src, b["by"].at[k])

    for t in both:
        raw_a(0, t)
    for t in both:
        raw_b(2, t)
    for t in both:
        raw_a_alone(0, t)
    for k in (3, 1):
        for t in both:
            raw_b(k, t)

    own_a, own_b, params = {}, {}, []
    for side in (0, 1):
        for j in (0, 1):
            for t in both:
                cut = delta[t].at[rows_a[t], parts[t].window(owner(1 - side, (1 - j) * s[t]))]
                own_a[t, j, side] = start_local(cut, bufs[t]["own_a"].at[j, side])
    for k in range(4):
        for t in both:
            cut = delta[t].at[rows_b[t], parts[t].window(owner(0, k * s[t]))]
            own_b[t, k] = start_local(cut, bufs[t]["own_b"].at[k])
    for t in both:
        params.append(start_local(master[t], master_next[t]))
        params.append(start_local(moment[t], moment_next[t]))

    tell(0)
    for t in both:
        merge_a(0, t)
    told(0)
    tell(1)
    for t in both:
        raw_a(1, t)
    for t in both:
        raw_a_alone(1, t)
    for t in both:
        b = bufs[t]
        arrived("by", 2, t)
        own_b[t, 2].wait()
        add_up(b["sum_b"].at[0], b["own_b"].at[2], b["by"].at[2])
        along_z(("b2", t), b["sum_b"].at[0], b["b2"], s[t])
    told(1)
    tell(2)
    for t in both:
        b = bufs[t]
        arrived("by", 3, t)
        own_b[t, 3].wait()
        add_up(b["sum_b"].at[1], b["own_b"].at[3], b["by"].at[3])
        along_z(("b1", t), b["sum_b"].at[1], b["b1"], -s[t])
    told(2)
    tell(3)
    for t in both:
        b = bufs[t]
        arrived("a1", 0, t)
        arrived("am", 0, t)
        own_a[t, 1, 0].wait()
        add_up(b["sum_a"], b["own_a"].at[1, 0], b["a1"].at[0], b["am"].at[0])
        along_y(("ay", t), b["sum_a"], b["ay"])
    for t in both:
        raw_b(0, t)
    told(3)
    tell(4)
    for t in both:
        merge_a(1, t)
    told(4)
    for t in both:
        b = bufs[t]
        arrived("by", 1, t)
        arrived("b2", t)
        own_b[t, 1].wait()
        add_up(b["sum_b"].at[2], b["own_b"].at[1], b["by"].at[1], b["b2"])
        along_z(("bm", t), b["sum_b"].at[2], b["bm"], s[t])

    for copy in params:
        copy.wait()
    for t in both:

        def base(rows, _, t=t):
            master_next[t][rows, :] = master_next[t][rows, :] - 0.567 * moment_next[t][rows, :]

        over_rows(parts[t].rows, base)

    def early(name, t):
        b = bufs[t]
        for slot, dz in enumerate((s[t], -s[t])):
            along_z((name, slot, t), b[name], b["got_" + name].at[slot], dz)
        along_y((name, 2, t), b[name], b["got_" + name].at[2])

    for t in both:
        add_up(bufs[t]["u"], master_next[t])
    for t in both:
        early("u", t)

    line = jnp.zeros((1, 128), F32)
    for t in both:
        b, p = bufs[t], parts[t]
        arrived("a1", 1, t)
        arrived("am", 1, t)
        arrived("ay", t)
        own_a[t, 1, 1].wait()
        terms = (b["own_a"].at[1, 1], b["a1"].at[1], b["am"].at[1], b["ay"])
        line += add_up_squares(b["total"].at[rows_a[t]], *terms)
    for t in both:
        b, p = bufs[t], parts[t]
        arrived("by", 0, t)
        arrived("b1", t)
        arrived("bm", t)
        own_b[t, 0].wait()
        terms = (b["own_b"].at[0], b["by"].at[0], b["b1"], b["bm"])
        line += add_up_squares(b["total"].at[rows_b[t]], *terms)

    line1[core] = line
    send(("n1",), line1.at[core], line1.at[core], chip(dc=1))
    arrived("n1")
    here = (x * 4 + y_hi * 2 + y_lo) * 4 + z
    line2[here] = jnp.sum(line1[...], axis=0)
    others = [(dx, dy, dz) for dx in range(4) for dy in range(4) for dz in range(4)][1:]
    for dx, dy, dz in others:
        send(("n2", dx, dy, dz), line2.at[here], line2.at[here], chip(dx=dx, dy=dy, dz=dz))
    for t in both:
        add_up(bufs[t]["v"], bufs[t]["total"])
    for t in both:
        early("v", t)
    for there in others:
        arrived("n2", *there)
    square_sum = jnp.sum(jnp.sum(line2[...], axis=0), axis=1, keepdims=True) * (1.0 / 64.0)
    factor = jnp.minimum(1.0, LIMIT / jnp.sqrt(square_sum + 1e-06)) * 0.125

    scale = 1.33 * factor

    def update(t, first, count, weights_too):
        b = bufs[t]
        mine = parts[t].window(rep)

        def body(rows, _):
            rows = pl.ds(pl.multiple_of(first + rows.start, STEP), STEP)
            new = master_next[t][rows, :] - scale * b["total"][rows, :]
            master_next[t][rows, :] = new
            if weights_too:
                weights[t][rows, mine] = new.astype(BF16)

        over_rows(count, body)

    def next_moment(t):
        b, m = bufs[t], moment_next[t]

        def body(rows, _):
            m[rows, :] = 0.9 * m[rows, :] + factor * b["total"][rows, :]

        over_rows(parts[t].rows, body)

    def work_out(t, u, v, who):
        columns = parts[t].window(owner(*who))

        def body(rows, _):
            new = u[rows, :].astype(F32) - scale * v[rows, :].astype(F32)
            weights[t][rows, columns] = new.astype(BF16)

        over_rows(parts[t].g, body)

    def work_out_got(t, slot, who):
        arrived("u", slot, t)
        arrived("v", slot, t)
        work_out(t, bufs[t]["got_u"].at[slot], bufs[t]["got_v"].at[slot], who)

    def give(t, rows, dz, who):
        place = weights[t].at[rows, parts[t].window(owner(*who))]
        key = ("w", t, rows.start, rows.size, dz, who)
        if dz is None:
            along_y(key, place, place)
        else:
            along_z(key, place, place, dz)

    def got(t, rows, dz, who):
        arrived("w", t, rows.start, rows.size, dz, who)

    own = (0, 0)
    for t in both:
        update(t, parts[t].g, parts[t].a - parts[t].g, True)
        give(t, rows_h[t], None, own)
    for t in both:
        update(t, parts[t].a, parts[t].b, True)
        for dz in (s[t], -s[t]):
            give(t, rows_b[t], dz, own)
    for t in both:
        give(t, rows_b[t], None, own)
    for t in both:
        for dz in (s[t], -s[t]):
            give(t, rows_h[t], dz, own)
    for t in both:
        work_out_got(t, 0, (0, -s[t]))
        give(t, rows_g[t], s[t], (0, -s[t]))
    for t in both:
        work_out_got(t, 2, (1, 0))
        for dz in (s[t], -s[t]):
            give(t, rows_g[t], dz, (1, 0))

    for t in both:
        got(t, rows_b[t], s[t], own)
        give(t, rows_b[t], s[t], (0, -s[t]))
        give(t, rows_b[t], None, (0, -s[t]))
    for t in both:
        got(t, rows_b[t], -s[t], own)
        give(t, rows_b[t], None, (0, s[t]))
    for t in both:
        got(t, rows_h[t], None, own)
        for dz in (s[t], -s[t]):
            give(t, rows_h[t], dz, (1, 0))
    for t in both:
        got(t, rows_h[t], s[t], own)
        give(t, rows_h[t], s[t], (0, -s[t]))
    for t in both:
        work_out(t, bufs[t]["u"], bufs[t]["v"], own)
        work_out_got(t, 1, (0, s[t]))
    for t in both:
        update(t, 0, parts[t].g, False)
        next_moment(t)
    for t in both:
        got(t, rows_b[t], s[t], (0, -s[t]))
        give(t, rows_b[t], None, (0, 2))
    for t in both:
        got(t, rows_g[t], s[t], (1, 0))
        got(t, rows_h[t], s[t], (1, 0))
        give(t, rows_a[t], s[t], (1, -s[t]))
    for t in both:
        got(t, rows_h[t], -s[t], own)
        got(t, rows_g[t], -s[t], (1, 0))
        got(t, rows_h[t], -s[t], (1, 0))
        got(t, rows_g[t], s[t], (0, -s[t]))
        got(t, rows_h[t], s[t], (0, -s[t]))
        got(t, rows_a[t], s[t], (1, -s[t]))
        for who in (own, (0, -s[t]), (0, s[t]), (0, 2)):
            got(t, rows_b[t], None, who)
    for copy in flying.values():
        copy.wait_send()


def shapes(p):
    a, b, g, c = p.a, p.b, p.g, p.columns
    return {
        "own_a": (2, 2, a, c),
        "own_b": (4, b, c),
        "a2": (2, a, c),
        "a1": (2, a, c),
        "am": (2, a, c),
        "ay": (a, c),
        "merged_a": (2, a, c),
        "sum_a": (a, c),
        "by": (4, b, c),
        "b2": (b, c),
        "b1": (b, c),
        "bm": (b, c),
        "sum_b": (3, b, c),
        "u": (g, c),
        "v": (g, c),
        "got_u": (3, g, c),
        "got_v": (3, g, c),
        "total": (p.rows, c),
    }


def scratch(p):
    return [pltpu.VMEM(shape, F32 if n == "total" else BF16) for n, shape in shapes(p).items()]


def write_out(*refs):
    count = len(refs) // 2
    copies = [pltpu.make_async_copy(refs[i], refs[count + i], refs[-1].at[i]) for i in range(count)]
    for copy in copies:
        copy.start()
    for copy in copies:
        copy.wait()


def on_device(delta_query, delta_output, *params):
    deltas = (delta_query[0], delta_output[0])
    parts = (Part(*params[0].shape, 1), Part(*params[1].shape, -1))
    outs = [(d.shape, BF16) for d in deltas] + [(p.shape, F32) for p in params]
    in_hbm = pl.BlockSpec(memory_space=pltpu.HBM)
    in_vmem = pl.BlockSpec(memory_space=pltpu.VMEM)
    held = pl.pallas_call(
        functools.partial(kernel, parts),
        out_shape=[pltpu.VMEM(*out) for out in outs],
        in_specs=[in_hbm] * 6,
        out_specs=[in_vmem] * 6,
        scratch_shapes=[
            *scratch(parts[0]),
            *scratch(parts[1]),
            pltpu.VMEM((2, 1, 128), F32),
            pltpu.VMEM((64, 1, 128), F32),
            pltpu.SemaphoreType.REGULAR((5,)),
            pltpu.SemaphoreType.DMA((144,)),
            pltpu.SemaphoreType.DMA((144,)),
            pltpu.SemaphoreType.DMA((32,)),
        ],
        compiler_params=pltpu.CompilerParams(
            collective_id=0, has_side_effects=True, vmem_limit_bytes=44 << 20
        ),
        name="outer_step",
    )(*deltas, *params)
    return pl.pallas_call(
        write_out,
        out_shape=[jax.ShapeDtypeStruct(*out) for out in outs],
        in_specs=[in_vmem] * 6,
        out_specs=[in_hbm] * 6,
        scratch_shapes=[pltpu.SemaphoreType.DMA((6,))],
        compiler_params=pltpu.CompilerParams(vmem_limit_bytes=16 << 20),
        name="write_out",
    )(*held)


def solution(mesh):
    placed = P("fsdp", "rep")
    return jax.shard_map(
        on_device,
        mesh=mesh,
        in_specs=(P("rep", "fsdp", None),) * 2 + (placed,) * 4,
        out_specs=(P("fsdp", None),) * 2 + (placed,) * 4,
        check_vma=False,
    )
```

```python
import functools
import math

import jax
import jax.numpy as jnp
from jax import lax
from jax.experimental import pallas as pl
from jax.experimental.pallas import tpu as pltpu
from jax.sharding import PartitionSpec as P

MESH = pl.DeviceIdType.MESH
BF16, F32 = jnp.bfloat16, jnp.float32
LIMIT = 0.25 * math.sqrt(2.0 * 8192 * 4096)
FIRST_Z = 9 / 16
EARLY = 1 / 4
STEP = 16


class Part:
    def __init__(self, rows, columns, sign):
        self.rows, self.columns, self.sign = rows, columns, sign
        self.a = int(rows * FIRST_Z) // STEP * STEP
        self.b = rows - self.a
        self.g = int(rows * EARLY) // STEP * STEP

    def window(self, owner):
        return pl.ds(pl.multiple_of(owner * self.columns, self.columns), self.columns)


def over_rows(rows, body, carry=None):
    def step(i, carry):
        return body(pl.ds(pl.multiple_of(i * STEP, STEP), STEP), carry)

    return lax.fori_loop(0, rows // STEP, step, carry, unroll=2 if rows // STEP % 2 == 0 else 1)


def add_up(out, *terms):
    def body(rows, _):
        total = terms[0][rows, :].astype(F32)
        for term in terms[1:]:
            total = total + term[rows, :].astype(F32)
        out[rows, :] = total.astype(out.dtype)

    over_rows(out.shape[0], body)


def add_up_squares(out, *terms):
    def body(rows, squares):
        total = terms[0][rows, :].astype(F32)
        for term in terms[1:]:
            total = total + term[rows, :].astype(F32)
        out[rows, :] = total
        return squares + total * total

    columns = out.shape[1]
    squares = over_rows(out.shape[0], body, jnp.zeros((STEP, columns), F32))
    line = jnp.sum(squares, axis=0, keepdims=True)
    return functools.reduce(jnp.add, [line[:, k : k + 128] for k in range(0, columns, 128)])


def kernel(parts, *refs):
    delta, master, moment = refs[0:2], refs[2:4], refs[4:6]
    weights, master_next, moment_next = refs[6:8], refs[8:10], refs[10:12]
    at = 12
    bufs = []
    for p in parts:
        names = list(shapes(p))
        bufs.append(dict(zip(names, refs[at : at + len(names)])))
        at += len(names)
    line1, line2, links, send_sem, recv_sem, local_sem = refs[at:]

    rep, shard = lax.axis_index("rep"), lax.axis_index("fsdp")
    y_hi, z = rep // 4, lax.rem(rep, 4)
    x, y_lo, core = shard // 4, lax.rem(shard // 2, 2), lax.rem(shard, 2)

    def owner(across, dz):
        return (1 - y_hi if across else y_hi) * 4 + lax.rem(z + dz % 4, 4)

    def chip(dx=0, dy=0, dz=0, dc=0):
        y = lax.rem(y_hi * 2 + y_lo + dy, 4)
        there = lax.rem(x + dx, 4) * 4 + lax.rem(y, 2) * 2 + lax.rem(core + dc, 2)
        return (y // 2) * 4 + lax.rem(z + dz, 4), there

    flying, local = {}, []

    def send(key, src, dst, target):
        k = len(flying)
        flying[key] = pltpu.make_async_remote_copy(
            src, dst, send_sem.at[k], recv_sem.at[k], device_id=target, device_id_type=MESH
        )
        flying[key].start()

    def arrived(*key):
        flying[key].wait_recv()

    def along_z(key, src, dst, dz):
        send(key, src, dst, (owner(0, dz), shard))

    def along_y(key, src, dst):
        send(key, src, dst, (owner(1, 0), shard))

    def start_local(src, dst):
        copy = pltpu.make_async_copy(src, dst, local_sem.at[len(local)])
        copy.start()
        local.append(copy)
        return copy

    both = range(len(parts))
    rows_a = [pl.ds(0, p.a) for p in parts]
    rows_b = [pl.ds(p.a, p.b) for p in parts]
    rows_g = [pl.ds(0, p.g) for p in parts]
    rows_h = [pl.ds(p.g, p.a - p.g) for p in parts]
    s = [p.sign for p in parts]

    around = {"x": (chip(dx=1), chip(dx=3)), "y": (chip(dy=1), chip(dy=3)), "z": (chip(dz=1), chip(dz=3))}
    near = [*around["z"], chip(dy=2), chip(dc=1), *around["y"], *around["x"]]
    barrier = pltpu.get_barrier_semaphore()
    for target in near:
        pl.semaphore_signal(barrier, inc=1, device_id=target, device_id_type=MESH)
    pl.semaphore_wait(barrier, len(near))

    def tell(i):
        for target in around["xyyzz"[i]]:
            pl.semaphore_signal(links.at[i], inc=1, device_id=target, device_id_type=MESH)

    def told(i):
        pl.semaphore_wait(links.at[i], 2)

    def raw_a(side, t):
        p, b = parts[t], bufs[t]
        src = delta[t].at[rows_a[t], p.window(owner(1 - side, 2))]
        along_z(("a2", side, t), src, b["a2"].at[side], s[t])

    def raw_a_alone(side, t):
        p, b = parts[t], bufs[t]
        src = delta[t].at[rows_a[t], p.window(owner(1 - side, -s[t]))]
        along_z(("a1", side, t), src, b["a1"].at[side], -s[t])

    def merge_a(side, t):
        b = bufs[t]
        arrived("a2", side, t)
        own_a[t, 0, side].wait()
        add_up(b["merged_a"].at[side], b["own_a"].at[0, side], b["a2"].at[side])
        along_z(("am", side, t), b["merged_a"].at[side], b["am"].at[side], s[t])

    def raw_b(k, t):
        p, b = parts[t], bufs[t]
        src = delta[t].at[rows_b[t], p.window(owner(1, k * s[t]))]
        along_y(("by", k, t), src, b["by"].at[k])

    for t in both:
        raw_a(0, t)
    for t in both:
        raw_b(2, t)
    for t in both:
        raw_a_alone(0, t)
    for k in (3, 1):
        for t in both:
            raw_b(k, t)

    own_a, own_b, params = {}, {}, []
    for side in (0, 1):
        for j in (0, 1):
            for t in both:
                cut = delta[t].at[rows_a[t], parts[t].window(owner(1 - side, (1 - j) * s[t]))]
                own_a[t, j, side] = start_local(cut, bufs[t]["own_a"].at[j, side])
    for k in range(4):
        for t in both:
            cut = delta[t].at[rows_b[t], parts[t].window(owner(0, k * s[t]))]
            own_b[t, k] = start_local(cut, bufs[t]["own_b"].at[k])
    for t in both:
        params.append(start_local(master[t], master_next[t]))
        params.append(start_local(moment[t], moment_next[t]))

    tell(0)
    for t in both:
        merge_a(0, t)
    told(0)
    tell(1)
    for t in both:
        raw_a(1, t)
    for t in both:
        raw_a_alone(1, t)
    for t in both:
        b = bufs[t]
        arrived("by", 2, t)
        own_b[t, 2].wait()
        add_up(b["sum_b"].at[0], b["own_b"].at[2], b["by"].at[2])
        along_z(("b2", t), b["sum_b"].at[0], b["b2"], s[t])
    told(1)
    tell(2)
    for t in both:
        b = bufs[t]
        arrived("by", 3, t)
        own_b[t, 3].wait()
        add_up(b["sum_b"].at[1], b["own_b"].at[3], b["by"].at[3])
        along_z(("b1", t), b["sum_b"].at[1], b["b1"], -s[t])
    told(2)
    tell(3)
    for t in both:
        b = bufs[t]
        arrived("a1", 0, t)
        arrived("am", 0, t)
        own_a[t, 1, 0].wait()
        add_up(b["sum_a"], b["own_a"].at[1, 0], b["a1"].at[0], b["am"].at[0])
        along_y(("ay", t), b["sum_a"], b["ay"])
    for t in both:
        raw_b(0, t)
    told(3)
    tell(4)
    for t in both:
        merge_a(1, t)
    told(4)
    for t in both:
        b = bufs[t]
        arrived("by", 1, t)
        arrived("b2", t)
        own_b[t, 1].wait()
        add_up(b["sum_b"].at[2], b["own_b"].at[1], b["by"].at[1], b["b2"])
        along_z(("bm", t), b["sum_b"].at[2], b["bm"], s[t])

    for copy in params:
        copy.wait()
    for t in both:

        def base(rows, _, t=t):
            master_next[t][rows, :] = master_next[t][rows, :] - 0.567 * moment_next[t][rows, :]

        over_rows(parts[t].rows, base)

    def early(name, t):
        b = bufs[t]
        for slot, dz in enumerate((s[t], -s[t])):
            along_z((name, slot, t), b[name], b["got_" + name].at[slot], dz)
        along_y((name, 2, t), b[name], b["got_" + name].at[2])

    for t in both:
        add_up(bufs[t]["u"], master_next[t])
    for t in both:
        early("u", t)

    line = jnp.zeros((1, 128), F32)
    for t in both:
        b, p = bufs[t], parts[t]
        arrived("a1", 1, t)
        arrived("am", 1, t)
        arrived("ay", t)
        own_a[t, 1, 1].wait()
        terms = (b["own_a"].at[1, 1], b["a1"].at[1], b["am"].at[1], b["ay"])
        line += add_up_squares(b["total"].at[rows_a[t]], *terms)
    for t in both:
        b, p = bufs[t], parts[t]
        arrived("by", 0, t)
        arrived("b1", t)
        arrived("bm", t)
        own_b[t, 0].wait()
        terms = (b["own_b"].at[0], b["by"].at[0], b["b1"], b["bm"])
        line += add_up_squares(b["total"].at[rows_b[t]], *terms)

    line1[core] = line
    send(("n1",), line1.at[core], line1.at[core], chip(dc=1))
    for t in both:
        add_up(bufs[t]["v"], bufs[t]["total"])
    arrived("n1")
    here = (x * 4 + y_hi * 2 + y_lo) * 4 + z
    line2[here] = jnp.sum(line1[...], axis=0)
    others = [(dx, dy, dz) for dx in range(4) for dy in range(4) for dz in range(4)][1:]
    for k, (dx, dy, dz) in enumerate(others):
        if k == 15:
            for t in both:
                early("v", t)
        send(("n2", dx, dy, dz), line2.at[here], line2.at[here], chip(dx=dx, dy=dy, dz=dz))
    for there in others:
        arrived("n2", *there)
    square_sum = jnp.sum(jnp.sum(line2[...], axis=0), axis=1, keepdims=True) * (1.0 / 64.0)
    factor = jnp.minimum(1.0, LIMIT / jnp.sqrt(square_sum + 1e-06)) * 0.125

    scale = 1.33 * factor

    def update(t, first, count, weights_too):
        b = bufs[t]
        mine = parts[t].window(rep)

        def body(rows, _):
            rows = pl.ds(pl.multiple_of(first + rows.start, STEP), STEP)
            new = master_next[t][rows, :] - scale * b["total"][rows, :]
            master_next[t][rows, :] = new
            if weights_too:
                weights[t][rows, mine] = new.astype(BF16)

        over_rows(count, body)

    def next_moment(t):
        b, m = bufs[t], moment_next[t]

        def body(rows, _):
            m[rows, :] = 0.9 * m[rows, :] + factor * b["total"][rows, :]

        over_rows(parts[t].rows, body)

    def work_out(t, u, v, who):
        columns = parts[t].window(owner(*who))

        def body(rows, _):
            new = u[rows, :].astype(F32) - scale * v[rows, :].astype(F32)
            weights[t][rows, columns] = new.astype(BF16)

        over_rows(parts[t].g, body)

    def work_out_got(t, slot, who):
        arrived("u", slot, t)
        arrived("v", slot, t)
        work_out(t, bufs[t]["got_u"].at[slot], bufs[t]["got_v"].at[slot], who)

    def give(t, rows, dz, who):
        place = weights[t].at[rows, parts[t].window(owner(*who))]
        key = ("w", t, rows.start, rows.size, dz, who)
        if dz is None:
            along_y(key, place, place)
        else:
            along_z(key, place, place, dz)

    def got(t, rows, dz, who):
        arrived("w", t, rows.start, rows.size, dz, who)

    own = (0, 0)
    for t in both:
        update(t, parts[t].g, parts[t].a - parts[t].g, True)
        give(t, rows_h[t], None, own)
    for t in both:
        update(t, parts[t].a, parts[t].b, True)
        for dz in (s[t], -s[t]):
            give(t, rows_b[t], dz, own)
    for t in both:
        give(t, rows_b[t], None, own)
    for t in both:
        for dz in (s[t], -s[t]):
            give(t, rows_h[t], dz, own)
    for t in both:
        work_out_got(t, 0, (0, -s[t]))
        give(t, rows_g[t], s[t], (0, -s[t]))
    for t in both:
        work_out_got(t, 2, (1, 0))
        for dz in (s[t], -s[t]):
            give(t, rows_g[t], dz, (1, 0))

    for t in both:
        got(t, rows_b[t], s[t], own)
        give(t, rows_b[t], s[t], (0, -s[t]))
        give(t, rows_b[t], None, (0, -s[t]))
    for t in both:
        got(t, rows_b[t], -s[t], own)
        give(t, rows_b[t], None, (0, s[t]))
    for t in both:
        got(t, rows_h[t], None, own)
        for dz in (s[t], -s[t]):
            give(t, rows_h[t], dz, (1, 0))
    for t in both:
        got(t, rows_h[t], s[t], own)
        give(t, rows_h[t], s[t], (0, -s[t]))
    for t in both:
        work_out(t, bufs[t]["u"], bufs[t]["v"], own)
        work_out_got(t, 1, (0, s[t]))
    for t in both:
        update(t, 0, parts[t].g, False)
        next_moment(t)
    for t in both:
        got(t, rows_b[t], s[t], (0, -s[t]))
        give(t, rows_b[t], None, (0, 2))
    for t in both:
        got(t, rows_g[t], s[t], (1, 0))
        got(t, rows_h[t], s[t], (1, 0))
        give(t, rows_a[t], s[t], (1, -s[t]))
    for t in both:
        got(t, rows_h[t], -s[t], own)
        got(t, rows_g[t], -s[t], (1, 0))
        got(t, rows_h[t], -s[t], (1, 0))
        got(t, rows_g[t], s[t], (0, -s[t]))
        got(t, rows_h[t], s[t], (0, -s[t]))
        got(t, rows_a[t], s[t], (1, -s[t]))
        for who in (own, (0, -s[t]), (0, s[t]), (0, 2)):
            got(t, rows_b[t], None, who)
    for copy in flying.values():
        copy.wait_send()


def shapes(p):
    a, b, g, c = p.a, p.b, p.g, p.columns
    return {
        "own_a": (2, 2, a, c),
        "own_b": (4, b, c),
        "a2": (2, a, c),
        "a1": (2, a, c),
        "am": (2, a, c),
        "ay": (a, c),
        "merged_a": (2, a, c),
        "sum_a": (a, c),
        "by": (4, b, c),
        "b2": (b, c),
        "b1": (b, c),
        "bm": (b, c),
        "sum_b": (3, b, c),
        "u": (g, c),
        "v": (g, c),
        "got_u": (3, g, c),
        "got_v": (3, g, c),
        "total": (p.rows, c),
    }


def scratch(p):
    return [pltpu.VMEM(shape, F32 if n == "total" else BF16) for n, shape in shapes(p).items()]


def write_out(*refs):
    count = len(refs) // 2
    copies = [pltpu.make_async_copy(refs[i], refs[count + i], refs[-1].at[i]) for i in range(count)]
    for copy in copies:
        copy.start()
    for copy in copies:
        copy.wait()


def on_device(delta_query, delta_output, *params):
    deltas = (delta_query[0], delta_output[0])
    parts = (Part(*params[0].shape, 1), Part(*params[1].shape, -1))
    outs = [(d.shape, BF16) for d in deltas] + [(p.shape, F32) for p in params]
    in_hbm = pl.BlockSpec(memory_space=pltpu.HBM)
    in_vmem = pl.BlockSpec(memory_space=pltpu.VMEM)
    held = pl.pallas_call(
        functools.partial(kernel, parts),
        out_shape=[pltpu.VMEM(*out) for out in outs],
        in_specs=[in_hbm] * 6,
        out_specs=[in_vmem] * 6,
        scratch_shapes=[
            *scratch(parts[0]),
            *scratch(parts[1]),
            pltpu.VMEM((2, 1, 128), F32),
            pltpu.VMEM((64, 1, 128), F32),
            pltpu.SemaphoreType.REGULAR((5,)),
            pltpu.SemaphoreType.DMA((144,)),
            pltpu.SemaphoreType.DMA((144,)),
            pltpu.SemaphoreType.DMA((32,)),
        ],
        compiler_params=pltpu.CompilerParams(
            collective_id=0, has_side_effects=True, vmem_limit_bytes=44 << 20
        ),
        name="outer_step",
    )(*deltas, *params)
    return pl.pallas_call(
        write_out,
        out_shape=[jax.ShapeDtypeStruct(*out) for out in outs],
        in_specs=[in_vmem] * 6,
        out_specs=[in_hbm] * 6,
        scratch_shapes=[pltpu.SemaphoreType.DMA((6,))],
        compiler_params=pltpu.CompilerParams(vmem_limit_bytes=16 << 20),
        name="write_out",
    )(*held)


def solution(mesh):
    placed = P("fsdp", "rep")
    return jax.shard_map(
        on_device,
        mesh=mesh,
        in_specs=(P("rep", "fsdp", None),) * 2 + (placed,) * 4,
        out_specs=(P("fsdp", None),) * 2 + (placed,) * 4,
        check_vma=False,
    )
```
